32 devices in a mesh: groups: 2 (over x), tensor: 8 (over z, y), head: 2 (over core).
Axes of the slice: x: 2, y: 2, z: 4, core: 2. Of those that a mesh axis runs over, the one named last changes fastest.
Arguments:
- hidden_state: bfloat16 [64, 5120], P(('groups', 'tensor', 'head')), parts along dimension 0, may hold values from -6 to 6
- input_gain: float32 [5120], replicated, may hold values from 0.5 to 1.5
- w_qkv: bfloat16 [2, 5120, 5120], P('head', None, 'tensor'), may hold values from -0.078125 to 0.078125
- query_gain: float32 [128], replicated, may hold values from 0.1 to 1.9
- key_gain: float32 [128], replicated, may hold values from 0.1 to 1.9
- slot_of: int32 [64], P('groups'), parts along dimension 0, may hold values from 0 to 31, each once
- lengths: int32 [64], P(('groups', 'tensor')), parts along dimension 0, may hold values from 1 to 384, 6144 in all
- key_cache: bfloat16 [64, 8, 384, 128], P(('groups', 'tensor'), 'head'), parts along dimension 0, may hold values from -127 to 127
- value_cache: bfloat16 [64, 8, 384, 128], P(('groups', 'tensor'), 'head'), parts along dimension 0, may hold values from -127 to 127
- key_scale: float32 [64, 8, 3], P(('groups', 'tensor'), 'head'), parts along dimension 0, may hold values from 0.003 to 1
- value_scale: float32 [64, 8, 3], P(('groups', 'tensor'), 'head'), parts along dimension 0, may hold values from 0.01 to 0.1
- w_out: bfloat16 [2, 4096, 5120], P('head', 'tensor'), may hold values from -0.0625 to 0.0625
- middle_gain: float32 [5120], replicated, may hold values from 0.5 to 1.5
- w_gate: bfloat16 [5120, 25600], P(None, ('tensor', 'head')), may hold values from -0.078125 to 0.078125
- w_up: bfloat16 [5120, 25600], P(None, ('tensor', 'head')), may hold values from -0.078125 to 0.078125
- w_down: bfloat16 [25600, 5120], P(('tensor', 'head')), may hold values from -0.0390625 to 0.0390625
Outputs:
- layer_out: bfloat16 [64, 5120], P(('groups', 'tensor', 'head')), parts along dimension 0
- new_kv: bfloat16 [64, 2, 8, 128], P(('groups', 'tensor'), None, 'head'), parts along dimension 0
The draws below stay inside these ranges and needn't reach their ends.
There are 2 independent parts, one for each index of `groups`. The reference program is written for one: setup_inputs(seed, part) draws one part's arguments, and reference() takes and returns one part's arrays. A program takes and returns all parts, laid end to end along the dimension named above; an argument that names none is the same for every part. Nothing has to cross between parts.
Inputs may be any that keep to these rules, and one draw needn't show every extreme that they name: A permutation: request r's cache lives in slot slot_of[r]. `lengths`: the largest is exactly 384 in every draw; in each part they sum to 6144.
All inputs are finite; a program needn't handle non-finite values. No bound on the sum of `lengths` on one device may be relied on, other than what follows from the above.
Results may differ from the reference program's by a relative error of at most 0.018.
The reference program's roundings to bfloat16 on the way count: a program that leaves them out, or rounds other values in their place, can miss the bound.
Values may be sent and summed in bfloat16 or wider, within the bound.
A program may use at most 128 MiB of HBM per device.

```python
import math
import jax
import jax.numpy as jnp
import numpy as np
from jax import lax

D = 5120
HEADS = 64
KVH = 8
HD = 128
FF = 25600
CACHE_LEN = 384
GROUP = 8
REQUESTS = 32
QKV_HALF = 5120
NBLK = 3


def draw_key_scale(key, part):
    lower_end = math.log(0.003)
    upper_end = math.log(0.03)
    uniform_draw = jax.random.uniform(key, (REQUESTS, KVH, NBLK), jnp.float32)
    return jnp.exp(lower_end + uniform_draw * (upper_end - lower_end))


def levels(stream_key, shape, split, least, largest):
    factor_of, own = 1.0, jax.random.fold_in(stream_key, 6)
    for position, shards_of in split:
        draws = jnp.exp(jax.random.uniform(jax.random.fold_in(own, position), (shards_of,), jnp.float32, least / len(split), largest / len(split)))
        factor_of = factor_of * jnp.repeat(draws, shape[position] // shards_of).reshape([-1 if axis == position else 1 for axis in range(len(shape))])
    return factor_of


def split_up(number_of, total, most, lean):
    portions = [(1 << 20) // math.isqrt(rank ** lean) + 1 for rank in range(2, number_of + 1)]
    rest, given = total - most - (number_of - 1), [1] * (number_of - 1)
    while rest > 0:
        movable = [i for i in range(number_of - 1) if given[i] < most]
        pool, remaining = sum([portions[i] for i in movable]), rest
        for i in movable:
            more = min(most - given[i], max(1, remaining * portions[i] // pool), rest)
            given[i] = given[i] + more
            rest = rest - more
    return np.array([most] + given)


def uneven(key, number_of, total, most, lean):
    if number_of == 2:
        one = jax.random.randint(key, (), max(1, total - most), min(most, total - 1) + 1)
        return jnp.stack([one, total - one])
    tallies = jnp.asarray(split_up(number_of, total, most, lean), jnp.int32)
    pairs = (number_of - 1) // 2
    source_of, receiver = tallies[1:1 + 2 * pairs:2], tallies[2:2 + 2 * pairs:2]
    room = jnp.minimum(source_of - 1, most - receiver)
    shifted = jax.random.randint(jax.random.fold_in(key, 1), (pairs,), 0, 1 << 20) % (room + 1)
    tallies = tallies.at[1:1 + 2 * pairs:2].set(source_of - shifted).at[2:2 + 2 * pairs:2].set(receiver + shifted)
    return tallies[jax.random.permutation(jax.random.fold_in(key, 2), number_of)]


def gaussian(rng, dims, scale, bound, split=(), held_as=jnp.bfloat16):
    array = scale * jax.random.normal(rng, dims, jnp.float32)
    if split:
        array = array * levels(rng, dims, split, -0.22, 0.18)
    return jnp.clip(array, -bound, bound).astype(held_as)


def setup_inputs(seed: int = 0, part: int = 0) -> dict:
    key_list = jax.random.split(jax.random.key(seed), 17)
    own_keys = jax.random.split(jax.random.fold_in(key_list[16], part), 17)
    hidden_state = gaussian(own_keys[0], (REQUESTS, D), 1.0, 6.0, ((0, 16),))
    input_gain = jnp.clip(1.0 + 0.1 * jax.random.normal(key_list[1], (D,), jnp.float32), 0.5, 1.5)
    w_qkv = gaussian(key_list[2], (2, D, QKV_HALF), D ** -0.5, 0.078125, ((0, 2), (2, 8)))
    query_gain = jnp.clip(1.0 + 0.18 * jax.random.normal(key_list[3], (HD,), jnp.float32), 0.1, 1.9)
    key_gain = jnp.clip(1.0 + 0.18 * jax.random.normal(key_list[4], (HD,), jnp.float32), 0.1, 1.9)
    slot_of = jax.random.permutation(own_keys[5], REQUESTS).astype(jnp.int32)
    lengths = uneven(own_keys[6], REQUESTS, REQUESTS * CACHE_LEN // 2, CACHE_LEN, 2).astype(jnp.int32)
    key_cache = jnp.clip(jax.random.uniform(own_keys[7], (REQUESTS, KVH, CACHE_LEN, HD), jnp.float32, -127.0, 127.0) * levels(own_keys[7], (REQUESTS, KVH, CACHE_LEN, HD), ((0, 8), (1, 2)), -0.4, 0.0), -127.0, 127.0).astype(jnp.bfloat16)
    value_cache = jnp.clip(jax.random.uniform(own_keys[8], (REQUESTS, KVH, CACHE_LEN, HD), jnp.float32, -127.0, 127.0) * levels(own_keys[8], (REQUESTS, KVH, CACHE_LEN, HD), ((0, 8), (1, 2)), -0.4, 0.0), -127.0, 127.0).astype(jnp.bfloat16)
    key_scale = draw_key_scale(jax.random.fold_in(jax.random.fold_in(key_list[16], part), 71), part)
    value_scale = jnp.clip(jnp.exp(math.log(0.1) - 2.3025851 * jax.random.uniform(own_keys[10], (REQUESTS, KVH, NBLK), jnp.float32) ** levels(own_keys[10], (REQUESTS, KVH, NBLK), ((0, 8), (1, 2)), -0.2, 0.2)), 0.01, 0.1)
    w_out = gaussian(key_list[11], (2, HEADS * HD // 2, D), (HEADS * HD) ** -0.5, 0.0625, ((0, 2), (1, 8)))
    middle_gain = jnp.clip(1.0 + 0.1 * jax.random.normal(key_list[12], (D,), jnp.float32), 0.5, 1.5)
    w_gate = gaussian(key_list[13], (D, FF), D ** -0.5, 0.078125, ((1, 16),))
    w_up = gaussian(key_list[14], (D, FF), D ** -0.5, 0.078125, ((1, 16),))
    w_down = gaussian(key_list[15], (FF, D), FF ** -0.5, 0.0390625, ((0, 16),))
    return {"hidden_state": hidden_state, "input_gain": input_gain, "w_qkv": w_qkv, "query_gain": query_gain, "key_gain": key_gain, "slot_of": slot_of, "lengths": lengths, "key_cache": key_cache, "value_cache": value_cache, "key_scale": key_scale, "value_scale": value_scale, "w_out": w_out, "middle_gain": middle_gain, "w_gate": w_gate, "w_up": w_up, "w_down": w_down}


EPSILON = 1e-06
THETA = 1000000.0

def rms_scale(values, gain_vector):
    mean_square = lax.optimization_barrier(jnp.mean(values * values, axis=-1, keepdims=True))
    return values * lax.rsqrt(mean_square + EPSILON) * gain_vector

def rotate(values, positions):
    full_width = values.shape[-1]
    half_width = full_width // 2
    frequency = jnp.power(jnp.float32(THETA), -jnp.arange(half_width, dtype=jnp.float32) * 2.0 / full_width)
    angles = positions.astype(jnp.float32)[..., None] * frequency
    cosine = jnp.cos(angles)
    sine_part = jnp.sin(angles)
    lower_half = values[..., :half_width]
    upper_half = values[..., half_width:]
    return jnp.concatenate([lower_half * cosine - upper_half * sine_part, upper_half * cosine + lower_half * sine_part], axis=-1)

def attend_slot(operands):
    query_rot, key_rot, values_new, key_codes, value_codes, key_scales, value_scales, cached = operands
    block_size = key_codes.shape[1] // key_scales.shape[1]
    inverse_root = 1.0 / math.sqrt(query_rot.shape[-1])
    key_expand = jnp.repeat(key_scales, block_size, axis=1)
    value_expand = jnp.repeat(value_scales, block_size, axis=1)
    raw_scores = jnp.einsum('gih,gph->gip', query_rot.astype(jnp.float32), key_codes.astype(jnp.float32))
    positions = jnp.arange(key_codes.shape[1], dtype=jnp.int32)
    live_mask = positions < cached
    cache_scores = jnp.where(live_mask, raw_scores * key_expand[:, None, :] * inverse_root, -jnp.inf)
    own_scores = jnp.einsum('gih,gh->gi', query_rot.astype(jnp.float32), key_rot.astype(jnp.float32)) * inverse_root
    highest = jnp.maximum(lax.optimization_barrier(jnp.max(cache_scores, axis=-1)), own_scores)
    cache_exp = jnp.exp(cache_scores - highest[..., None])
    own_exp = jnp.exp(own_scores - highest)
    denominator = lax.optimization_barrier(jnp.sum(cache_exp, axis=-1)) + own_exp
    cache_weights = (cache_exp * value_expand[:, None, :] / denominator[..., None]).astype(jnp.bfloat16)
    own_weights = (own_exp / denominator).astype(jnp.bfloat16)
    mixed_sum = jnp.einsum('gip,gph->gih', cache_weights.astype(jnp.float32), value_codes.astype(jnp.float32))
    mixed_sum = mixed_sum + own_weights.astype(jnp.float32)[..., None] * values_new.astype(jnp.float32)[:, None, :]
    return mixed_sum.astype(jnp.bfloat16)

def reference(hidden_state, input_gain, w_qkv, query_gain, key_gain, slot_of, lengths, key_cache, value_cache, key_scale, value_scale, w_out, middle_gain, w_gate, w_up, w_down):
    normed_in = rms_scale(hidden_state.astype(jnp.float32), input_gain).astype(jnp.bfloat16)
    halves = [jnp.dot(normed_in, w_qkv[half_index], preferred_element_type=jnp.float32) for half_index in range(2)]
    qkv_all = jnp.stack(halves).astype(jnp.bfloat16)
    request_of = jnp.zeros((REQUESTS,), jnp.int32).at[slot_of].set(jnp.arange(REQUESTS, dtype=jnp.int32))
    by_slot = qkv_all[:, request_of]
    grouped = by_slot.reshape(2, REQUESTS, KVH // 2, GROUP + 2, HD).transpose(1, 0, 2, 3, 4).reshape(REQUESTS, KVH, GROUP + 2, HD)
    queries = grouped[:, :, :GROUP].astype(jnp.float32)
    keys_new = grouped[:, :, GROUP].astype(jnp.float32)
    values_new = grouped[:, :, GROUP + 1]
    query_rot = rotate(rms_scale(queries, query_gain), lengths[:, None, None]).astype(jnp.bfloat16)
    key_rot = rotate(rms_scale(keys_new, key_gain), lengths[:, None]).astype(jnp.bfloat16)
    new_kv = jnp.stack([key_rot, values_new], axis=1)
    attended = lax.map(attend_slot, (query_rot, key_rot, values_new, key_cache, value_cache, key_scale, value_scale, lengths))
    by_request = attended.reshape(REQUESTS, HEADS * HD)[slot_of]
    projected = jnp.dot(by_request, w_out.reshape(HEADS * HD, D), preferred_element_type=jnp.float32)
    middle = (hidden_state.astype(jnp.float32) + projected).astype(jnp.bfloat16)
    normed_mid = rms_scale(middle.astype(jnp.float32), middle_gain).astype(jnp.bfloat16)
    gate_part = jnp.dot(normed_mid, w_gate, preferred_element_type=jnp.float32)
    up_part = jnp.dot(normed_mid, w_up, preferred_element_type=jnp.float32)
    activation = (jax.nn.silu(gate_part) * up_part).astype(jnp.bfloat16)
    layer_out = (middle.astype(jnp.float32) + jnp.dot(activation, w_down, preferred_element_type=jnp.float32)).astype(jnp.bfloat16)
    return (layer_out, new_kv)
```

```python
import functools
import math

import jax
import jax.numpy as jnp
from jax import lax
from jax.experimental import pallas as pl
from jax.experimental.pallas import tpu as pltpu
from jax.sharding import PartitionSpec as P

EPSILON = 1e-06
THETA = 1000000.0


def rms_scale(values, gain_vector):
    mean_square = jnp.mean(values * values, axis=-1, keepdims=True)
    return values * lax.rsqrt(mean_square + EPSILON) * gain_vector


def rotate(values, positions):
    full_width = values.shape[-1]
    half_width = full_width // 2
    frequency = jnp.power(
        jnp.float32(THETA), -jnp.arange(half_width, dtype=jnp.float32) * 2.0 / full_width
    )
    angles = positions.astype(jnp.float32)[..., None] * frequency
    cosine = jnp.cos(angles)
    sine_part = jnp.sin(angles)
    lower_half = values[..., :half_width]
    upper_half = values[..., half_width:]
    return jnp.concatenate(
        [
            lower_half * cosine - upper_half * sine_part,
            upper_half * cosine + lower_half * sine_part,
        ],
        axis=-1,
    )


def gate_units(normed_rows, w_gate, w_up):
    gate_part = jnp.dot(normed_rows, w_gate, preferred_element_type=jnp.float32)
    up_part = jnp.dot(normed_rows, w_up, preferred_element_type=jnp.float32)
    return (jax.nn.silu(gate_part) * up_part).astype(jnp.bfloat16)


def softmax_weights(cache_scores, own_scores, value_expand):
    highest = jnp.maximum(jnp.max(cache_scores, axis=-1), own_scores)
    cache_exp = jnp.exp(cache_scores - highest[..., None])
    own_exp = jnp.exp(own_scores - highest)
    denominator = jnp.sum(cache_exp, axis=-1) + own_exp
    cache_weights = (cache_exp * value_expand[:, :, None, :] / denominator[..., None]).astype(
        jnp.bfloat16
    )
    own_weights = (own_exp / denominator).astype(jnp.bfloat16)
    return (cache_weights, own_weights)


MESH_ID = pl.DeviceIdType.MESH
VMEM_LIMIT = 66_500_000


def remote(src, dst, send_sem, recv_sem, tensor_index, head_index):
    return pltpu.make_async_remote_copy(
        src_ref=src,
        dst_ref=dst,
        send_sem=send_sem,
        recv_sem=recv_sem,
        device_id={"tensor": tensor_index, "head": head_index},
        device_id_type=MESH_ID,
    )


def greet(mt, mh, nt):
    barrier = pltpu.get_barrier_semaphore()
    for k in range(1, nt):
        pl.semaphore_signal(
            barrier,
            inc=1,
            device_id={"tensor": lax.rem(mt + k, nt), "head": mh},
            device_id_type=MESH_ID,
        )
    pl.semaphore_signal(
        barrier, inc=1, device_id={"tensor": mt, "head": 1 - mh}, device_id_type=MESH_ID
    )
    pl.semaphore_wait(barrier, nt)


def gather_rows(own, gath, x32, sems, mt, mh, nt):
    send, recv, fsend, frecv = sems
    rows = own.shape[0]
    gath[mh, mt] = own
    copies = []
    for k in range(1, nt):
        copy = remote(
            gath.at[mh, mt], gath.at[mh, mt], send.at[k], recv.at[mt], lax.rem(mt + k, nt), mh
        )
        copy.start()
        copies.append(copy)
    copy = remote(gath.at[mh, mt], gath.at[mh, mt], fsend.at[mt], frecv.at[mt], mt, 1 - mh)
    copy.start()
    copies.append(copy)
    for k in range(1, nt):
        peer = lax.rem(mt + k, nt)
        block = gath.at[mh, peer]
        remote(block, block, send.at[k], recv.at[peer], mt, 1 - mh).wait_recv()
        copy = remote(block, block, fsend.at[peer], frecv.at[peer], mt, 1 - mh)
        copy.start()
        copies.append(copy)
    for t in range(nt):
        block = gath.at[1 - mh, t]
        remote(block, block, fsend.at[t], frecv.at[t], mt, 1 - mh).wait_recv()
    for copy in copies:
        copy.wait_send()
    for h in range(2):
        for t in range(nt):
            start = (h * nt + t) * rows
            x32[start : start + rows, :] = gath[h, t].astype(jnp.float32)


def scatter_sum(part, half, send2, recv2, sems, mt, mh, nt):
    psend, precv, send, recv = sems
    rows = send2.shape[1]
    swap = remote(part.at[1 - mh], half, psend.at[0], precv.at[0], mt, 1 - mh)
    swap.start()
    swap.wait_recv()
    for t in range(nt):
        span = slice(t * rows, (t + 1) * rows)
        send2[t] = (part[mh, span, :] + half[span, :]).astype(jnp.bfloat16)
    copies = []
    for k in range(1, nt):
        peer = lax.rem(mt + k, nt)
        copy = remote(send2.at[peer], recv2.at[mt], send.at[k], recv.at[mt], peer, mh)
        copy.start()
        copies.append(copy)
    total = send2[mt].astype(jnp.float32)
    for k in range(1, nt):
        peer = lax.rem(mt + k, nt)
        remote(send2.at[peer], recv2.at[peer], send.at[k], recv.at[peer], peer, mh).wait_recv()
        total = total + recv2[peer].astype(jnp.float32)
    swap.wait_send()
    for copy in copies:
        copy.wait_send()
    return total


def front_kernel(nt, chunks, hid, gain, slots, wq, out, wbuf, gath, x32, acc, snd, rcv, wsem, gsem, asem):
    mt = lax.axis_index("tensor")
    mh = lax.axis_index("head")
    depth = wq.shape[1] // chunks
    cols = wq.shape[2]
    for c in range(chunks):
        span = pl.ds(c * depth, depth)
        pltpu.make_async_copy(wq.at[0, span, :], wbuf.at[span, :], wsem.at[c]).start()
    greet(mt, mh, nt)
    own = rms_scale(hid[...].astype(jnp.float32), gain[...]).astype(jnp.bfloat16)
    gather_rows(own, gath, x32, [gsem.at[i] for i in range(4)], mt, mh, nt)
    acc[...] = jnp.zeros_like(acc)

    @pl.loop(0, chunks)
    def _(c):
        span = pl.ds(pl.multiple_of(c * depth, depth), depth)
        pltpu.make_async_copy(wq.at[0, span, :], wbuf.at[span, :], wsem.at[c]).wait()
        acc[...] += jnp.dot(
            x32[:, span].astype(jnp.bfloat16), wbuf[span, :], preferred_element_type=jnp.float32
        )

    requests = x32.shape[0]
    pick = jnp.where(
        lax.broadcasted_iota(jnp.int32, (requests, requests), 0) == slots[...], 1.0, 0.0
    ).astype(jnp.bfloat16)
    acc[...] = jnp.dot(pick, acc[...].astype(jnp.bfloat16), preferred_element_type=jnp.float32)
    per = requests // nt
    for t in range(nt):
        snd[t] = acc[t * per : (t + 1) * per, :].astype(jnp.bfloat16)
    copies = []
    for k in range(1, nt):
        peer = lax.rem(mt + k, nt)
        copy = remote(snd.at[peer], rcv.at[mt], asem.at[0, k], asem.at[1, mt], peer, mh)
        copy.start()
        copies.append(copy)
    rcv[mt] = snd[mt]
    for k in range(1, nt):
        peer = lax.rem(mt + k, nt)
        remote(snd.at[peer], rcv.at[peer], asem.at[0, k], asem.at[1, peer], peer, mh).wait_recv()
    for t in range(nt):
        out[:, t * cols : (t + 1) * cols] = rcv[t]
    for copy in copies:
        copy.wait_send()


def back_kernel(
    nt, chunks, att, slots, hid, gain, wo, wg, wu, wd, out,
    wob, wgb, wub, wdb, rcv, ret, part, half, send2, recv2, gath, x32, gacc, uacc,
    wsem, asem, gsem, ssem,
):
    mt = lax.axis_index("tensor")
    mh = lax.axis_index("head")
    width = wo.shape[2]
    tile = width // chunks
    depth = wg.shape[0] // chunks

    def column_copy(src, dst, i, c):
        span = pl.ds(pl.multiple_of(c * tile, tile), tile)
        return pltpu.make_async_copy(src.at[:, span], dst.at[:, span], wsem.at[i, c])

    def row_copy(src, dst, i, c):
        span = pl.ds(pl.multiple_of(c * depth, depth), depth)
        return pltpu.make_async_copy(src.at[span, :], dst.at[span, :], wsem.at[i, c])

    for c in range(chunks):
        column_copy(wo.at[0], wob, 0, c).start()
    for c in range(chunks):
        row_copy(wg, wgb, 1, c).start()
        row_copy(wu, wub, 2, c).start()
    for c in range(chunks):
        column_copy(wd, wdb, 3, c).start()
    greet(mt, mh, nt)
    copies = []
    for k in range(1, nt):
        peer = lax.rem(mt + k, nt)
        copy = remote(att.at[peer], rcv.at[mt], asem.at[0, k], asem.at[1, mt], peer, mh)
        copy.start()
        copies.append(copy)
    rcv[mt] = att[mt]
    for k in range(1, nt):
        peer = lax.rem(mt + k, nt)
        remote(att.at[peer], rcv.at[peer], asem.at[0, k], asem.at[1, peer], peer, mh).wait_recv()
    per = att.shape[1]
    for t in range(nt):
        ret[t * per : (t + 1) * per, :] = rcv[t].astype(jnp.float32)
    for copy in copies:
        copy.wait_send()
    requests = ret.shape[0]
    pick = jnp.where(
        lax.broadcasted_iota(jnp.int32, (requests, requests), 1) == slots[...], 1.0, 0.0
    ).astype(jnp.bfloat16)
    ret[...] = jnp.dot(pick, ret[...].astype(jnp.bfloat16), preferred_element_type=jnp.float32)
    middle_rows = requests // 2

    def column_dot(lhs, src, buf, i):
        @pl.loop(0, chunks)
        def _(c):
            column_copy(src, buf, i, c).wait()
            span = pl.ds(pl.multiple_of(c * tile, tile), tile)
            value = jnp.dot(lhs, buf[:, span], preferred_element_type=jnp.float32)
            part[0, :, span] = value[:middle_rows]
            part[1, :, span] = value[middle_rows:]

    column_dot(ret[...].astype(jnp.bfloat16), wo.at[0], wob, 0)
    summed = scatter_sum(
        part, half.at[0], send2.at[0], recv2.at[0], [ssem.at[0, i] for i in range(4)], mt, mh, nt
    )
    middle = (summed + hid[...].astype(jnp.float32)).astype(jnp.bfloat16)
    middle32 = middle.astype(jnp.float32)
    normed = rms_scale(middle32, gain[...]).astype(jnp.bfloat16)
    gather_rows(normed, gath, x32, [gsem.at[i] for i in range(4)], mt, mh, nt)
    gacc[...] = jnp.zeros_like(gacc)
    uacc[...] = jnp.zeros_like(uacc)

    @pl.loop(0, chunks)
    def _(c):
        span = pl.ds(pl.multiple_of(c * depth, depth), depth)
        rows = x32[:, span].astype(jnp.bfloat16)
        row_copy(wg, wgb, 1, c).wait()
        gacc[...] += jnp.dot(rows, wgb[span, :], preferred_element_type=jnp.float32)
        row_copy(wu, wub, 2, c).wait()
        uacc[...] += jnp.dot(rows, wub[span, :], preferred_element_type=jnp.float32)

    gate = gacc[...]
    activation = (gate / (1.0 + jnp.exp(-gate)) * uacc[...]).astype(jnp.bfloat16)
    gacc[...] = activation.astype(jnp.float32)
    column_dot(gacc[...].astype(jnp.bfloat16), wd, wdb, 3)
    summed = scatter_sum(
        part, half.at[1], send2.at[1], recv2.at[1], [ssem.at[1, i] for i in range(4)], mt, mh, nt
    )
    out[...] = (middle32 + summed).astype(jnp.bfloat16)


def front(nt, hidden_state, input_gain, slots_row, w_qkv):
    rows, width = hidden_state.shape
    requests = rows * nt * 2
    cols = w_qkv.shape[2]
    per = requests // nt
    chunks = 10
    vmem = pl.BlockSpec(memory_space=pltpu.VMEM)
    anyspace = pl.BlockSpec(memory_space=pl.ANY)
    dma = pltpu.SemaphoreType.DMA
    return pl.pallas_call(
        functools.partial(front_kernel, nt, chunks),
        out_shape=jax.ShapeDtypeStruct((per, cols * nt), jnp.bfloat16),
        in_specs=[vmem, vmem, vmem, anyspace],
        out_specs=vmem,
        scratch_shapes=[
            pltpu.VMEM((width, cols), jnp.bfloat16),
            pltpu.VMEM((2, nt, rows, width), jnp.bfloat16),
            pltpu.VMEM((requests, width), jnp.float32),
            pltpu.VMEM((requests, cols), jnp.float32),
            pltpu.VMEM((nt, per, cols), jnp.bfloat16),
            pltpu.VMEM((nt, per, cols), jnp.bfloat16),
            dma((chunks,)),
            dma((4, nt)),
            dma((2, nt)),
        ],
        compiler_params=pltpu.CompilerParams(
            collective_id=0, has_side_effects=True, vmem_limit_bytes=VMEM_LIMIT
        ),
    )(hidden_state, input_gain, slots_row, w_qkv)


def back(nt, attended, slots_column, hidden_state, middle_gain, w_out, w_gate, w_up, w_down):
    rows, width = hidden_state.shape
    requests = rows * nt * 2
    per = requests // nt
    cols = w_out.shape[1]
    units = w_gate.shape[1]
    chunks = 10
    vmem = pl.BlockSpec(memory_space=pltpu.VMEM)
    anyspace = pl.BlockSpec(memory_space=pl.ANY)
    dma = pltpu.SemaphoreType.DMA
    bf16, f32 = jnp.bfloat16, jnp.float32
    return pl.pallas_call(
        functools.partial(back_kernel, nt, chunks),
        out_shape=jax.ShapeDtypeStruct((rows, width), bf16),
        in_specs=[vmem] * 4 + [anyspace] * 4,
        out_specs=vmem,
        scratch_shapes=[
            pltpu.VMEM((cols, width), bf16),
            pltpu.VMEM((width, units), bf16),
            pltpu.VMEM((width, units), bf16),
            pltpu.VMEM((units, width), bf16),
            pltpu.VMEM((nt, per, cols), bf16),
            pltpu.VMEM((requests, cols), f32),
            pltpu.VMEM((2, requests // 2, width), f32),
            pltpu.VMEM((2, requests // 2, width), f32),
            pltpu.VMEM((2, nt, rows, width), bf16),
            pltpu.VMEM((2, nt, rows, width), bf16),
            pltpu.VMEM((2, nt, rows, width), bf16),
            pltpu.VMEM((requests, width), f32),
            pltpu.VMEM((requests, units), f32),
            pltpu.VMEM((requests, units), f32),
            dma((4, chunks)),
            dma((2, nt)),
            dma((4, nt)),
            dma((2, 4, nt)),
        ],
        compiler_params=pltpu.CompilerParams(
            collective_id=1, has_side_effects=True, vmem_limit_bytes=VMEM_LIMIT
        ),
    )(attended, slots_column, hidden_state, middle_gain, w_out, w_gate, w_up, w_down)


def kernels_fit(nt, nh, hidden_state, w_qkv, w_out, w_gate):
    width = hidden_state.shape[1]
    units = w_gate.shape[1]
    lanes = -(-units // 128) * 128
    weight_bytes = 2 * width * (w_out.shape[1] + 2 * lanes + units)
    other_bytes = 2 * nt * hidden_state.shape[0] * width * 24
    return (
        nh == 2
        and w_qkv.shape[2] % 128 == 0
        and w_out.shape[1] % 128 == 0
        and width % 1280 == 0
        and units % 16 == 0
        and weight_bytes + other_bytes < VMEM_LIMIT
    )


def per_device(
    nt,
    nh,
    hidden_state,
    input_gain,
    w_qkv,
    query_gain,
    key_gain,
    slot_of,
    lengths,
    key_cache,
    value_cache,
    key_scale,
    value_scale,
    w_out,
    middle_gain,
    w_gate,
    w_up,
    w_down,
):
    rows_local = hidden_state.shape[0]
    requests = slot_of.shape[0]
    fused = kernels_fit(nt, nh, hidden_state, w_qkv, w_out, w_gate)
    if fused:
        slots_by_head = slot_of.reshape(nt, nh, rows_local).transpose(1, 0, 2)
        owned_rows = front(
            nt,
            hidden_state,
            input_gain.reshape(1, -1),
            slots_by_head.reshape(1, requests),
            w_qkv,
        )
    else:
        normed_in = rms_scale(hidden_state.astype(jnp.float32), input_gain).astype(jnp.bfloat16)
        qkv_weights = w_qkv[0]
        qkv_local = jnp.dot(
            lax.all_gather(normed_in, ("tensor", "head"), axis=0, tiled=True),
            qkv_weights,
            preferred_element_type=jnp.float32,
        ).astype(jnp.bfloat16)
        request_of = (
            jnp.zeros((requests,), jnp.int32).at[slot_of].set(jnp.arange(requests, dtype=jnp.int32))
        )
        qkv_slots = jnp.take(qkv_local, request_of, axis=0)
        owned_rows = lax.all_to_all(qkv_slots, "tensor", split_axis=0, concat_axis=1, tiled=True)
    slots_here = owned_rows.shape[0]
    kv_local = key_cache.shape[1]
    cache_len = key_cache.shape[2]
    head_dim = key_cache.shape[3]
    block_size = cache_len // key_scale.shape[2]
    group_size = owned_rows.shape[1] // (kv_local * head_dim) - 2
    grouped = owned_rows.reshape(slots_here, kv_local, group_size + 2, head_dim)
    queries = grouped[:, :, :group_size].astype(jnp.float32)
    keys_new = grouped[:, :, group_size].astype(jnp.float32)
    values_new = grouped[:, :, group_size + 1]
    query_rot = rotate(rms_scale(queries, query_gain), lengths[:, None, None]).astype(jnp.bfloat16)
    key_rot = rotate(rms_scale(keys_new, key_gain), lengths[:, None]).astype(jnp.bfloat16)
    new_kv = jnp.stack([key_rot, values_new], axis=1)
    inverse_root = 1.0 / math.sqrt(head_dim)
    own_scores = (
        jnp.einsum("rgih,rgh->rgi", query_rot, key_rot, preferred_element_type=jnp.float32)
        * inverse_root
    )
    value_expand = jnp.repeat(value_scale, block_size, axis=2)
    key_expand = jnp.repeat(key_scale, block_size, axis=2)
    positions = jnp.arange(cache_len, dtype=jnp.int32)
    live_mask = positions[None, None, None, :] < lengths[:, None, None, None]
    raw_scores = jnp.einsum(
        "rgih,rgph->rgip", query_rot, key_cache, preferred_element_type=jnp.float32
    )
    cache_scores = jnp.where(
        live_mask, raw_scores * key_expand[:, :, None, :] * inverse_root, -jnp.inf
    )
    cache_weights, own_weights = softmax_weights(cache_scores, own_scores, value_expand)
    mixed_sum = jnp.einsum(
        "rgip,rgph->rgih", cache_weights, value_cache, preferred_element_type=jnp.float32
    )
    mixed_sum = (
        mixed_sum
        + own_weights.astype(jnp.float32)[..., None] * values_new.astype(jnp.float32)[:, :, None, :]
    )
    attended = mixed_sum.astype(jnp.bfloat16).reshape(slots_here, kv_local * group_size * head_dim)
    if fused:
        blocks = attended.reshape(slots_here, nt, -1).transpose(1, 0, 2)
        layer_out = back(
            nt,
            blocks,
            slots_by_head.reshape(requests, 1),
            hidden_state,
            middle_gain.reshape(1, -1),
            w_out,
            w_gate,
            w_up,
            w_down,
        )
        return (layer_out, new_kv)
    returned = lax.all_to_all(attended, "tensor", split_axis=1, concat_axis=0, tiled=True)
    by_request = jnp.take(returned, slot_of, axis=0)
    out_weights = w_out[0]
    own_offset = lax.axis_index(("tensor", "head")) * rows_local
    partial_out = jnp.dot(by_request, out_weights, preferred_element_type=jnp.float32)
    own_rows = lax.dynamic_slice_in_dim(
        partial_out, own_offset, rows_local, 0
    ) + hidden_state.astype(jnp.float32)
    with_residual = lax.dynamic_update_slice_in_dim(partial_out, own_rows, own_offset, 0)
    summed = lax.psum(with_residual, ("tensor", "head"))
    middle_all = summed.astype(jnp.bfloat16)
    normed_mid = rms_scale(middle_all.astype(jnp.float32), middle_gain).astype(jnp.bfloat16)
    activation = gate_units(normed_mid, w_gate, w_up)
    middle = lax.dynamic_slice_in_dim(middle_all, own_offset, rows_local, 0)
    reduced = lax.psum_scatter(
        jnp.dot(activation, w_down, preferred_element_type=jnp.float32),
        ("tensor", "head"),
        scatter_dimension=0,
        tiled=True,
    )
    layer_out = (middle.astype(jnp.float32) + reduced).astype(jnp.bfloat16)
    return (layer_out, new_kv)


def solution(mesh):
    return jax.shard_map(
        functools.partial(per_device, mesh.shape["tensor"], mesh.shape["head"]),
        mesh=mesh,
        in_specs=(
            P(("groups", "tensor", "head"), None),
            P(),
            P("head", None, "tensor"),
            P(),
            P(),
            P("groups"),
            P(("groups", "tensor")),
            P(("groups", "tensor"), "head", None, None),
            P(("groups", "tensor"), "head", None, None),
            P(("groups", "tensor"), "head", None),
            P(("groups", "tensor"), "head", None),
            P("head", "tensor", None),
            P(),
            P(None, ("tensor", "head")),
            P(None, ("tensor", "head")),
            P(("tensor", "head"), None),
        ),
        out_specs=(
            P(("groups", "tensor", "head"), None),
            P(("groups", "tensor"), None, "head", None),
        ),
        check_vma=False,
    )
```

```python
import functools
import math

import jax
import jax.numpy as jnp
from jax import lax
from jax.experimental import pallas as pl
from jax.experimental.pallas import tpu as pltpu
from jax.sharding import PartitionSpec as P

EPSILON = 1e-06
THETA = 1000000.0


def rms_scale(values, gain_vector):
    mean_square = jnp.mean(values * values, axis=-1, keepdims=True)
    return values * lax.rsqrt(mean_square + EPSILON) * gain_vector


def rotate(values, positions):
    full_width = values.shape[-1]
    half_width = full_width // 2
    frequency = jnp.power(
        jnp.float32(THETA), -jnp.arange(half_width, dtype=jnp.float32) * 2.0 / full_width
    )
    angles = positions.astype(jnp.float32)[..., None] * frequency
    cosine = jnp.cos(angles)
    sine_part = jnp.sin(angles)
    lower_half = values[..., :half_width]
    upper_half = values[..., half_width:]
    return jnp.concatenate(
        [
            lower_half * cosine - upper_half * sine_part,
            upper_half * cosine + lower_half * sine_part,
        ],
        axis=-1,
    )


def gate_units(normed_rows, w_gate, w_up):
    gate_part = jnp.dot(normed_rows, w_gate, preferred_element_type=jnp.float32)
    up_part = jnp.dot(normed_rows, w_up, preferred_element_type=jnp.float32)
    return (jax.nn.silu(gate_part) * up_part).astype(jnp.bfloat16)


def softmax_weights(cache_scores, own_scores, value_expand):
    highest = jnp.maximum(jnp.max(cache_scores, axis=-1), own_scores)
    cache_exp = jnp.exp(cache_scores - highest[..., None])
    own_exp = jnp.exp(own_scores - highest)
    denominator = jnp.sum(cache_exp, axis=-1) + own_exp
    cache_weights = (cache_exp * value_expand[:, :, None, :] / denominator[..., None]).astype(
        jnp.bfloat16
    )
    own_weights = (own_exp / denominator).astype(jnp.bfloat16)
    return (cache_weights, own_weights)


MESH_ID = pl.DeviceIdType.MESH
VMEM_LIMIT = 66_500_000


def remote(src, dst, send_sem, recv_sem, tensor_index, head_index):
    return pltpu.make_async_remote_copy(
        src_ref=src,
        dst_ref=dst,
        send_sem=send_sem,
        recv_sem=recv_sem,
        device_id={"tensor": tensor_index, "head": head_index},
        device_id_type=MESH_ID,
    )


def greet(mt, mh, nt):
    barrier = pltpu.get_barrier_semaphore()
    for k in range(1, nt):
        pl.semaphore_signal(
            barrier,
            inc=1,
            device_id={"tensor": lax.rem(mt + k, nt), "head": mh},
            device_id_type=MESH_ID,
        )
    pl.semaphore_signal(
        barrier, inc=1, device_id={"tensor": mt, "head": 1 - mh}, device_id_type=MESH_ID
    )
    pl.semaphore_wait(barrier, nt)


def gather_rows(own, gath, x32, sems, mt, mh, nt):
    send, recv, fsend, frecv = sems
    rows = own.shape[0]
    gath[mh, mt] = own
    copies = []
    for k in range(1, nt):
        copy = remote(
            gath.at[mh, mt], gath.at[mh, mt], send.at[k], recv.at[mt], lax.rem(mt + k, nt), mh
        )
        copy.start()
        copies.append(copy)
    copy = remote(gath.at[mh, mt], gath.at[mh, mt], fsend.at[mt], frecv.at[mt], mt, 1 - mh)
    copy.start()
    copies.append(copy)
    for k in range(1, nt):
        peer = lax.rem(mt + k, nt)
        block = gath.at[mh, peer]
        remote(block, block, send.at[k], recv.at[peer], mt, 1 - mh).wait_recv()
        copy = remote(block, block, fsend.at[peer], frecv.at[peer], mt, 1 - mh)
        copy.start()
        copies.append(copy)
    for t in range(nt):
        block = gath.at[1 - mh, t]
        remote(block, block, fsend.at[t], frecv.at[t], mt, 1 - mh).wait_recv()
    for copy in copies:
        copy.wait_send()
    for h in range(2):
        for t in range(nt):
            start = (h * nt + t) * rows
            x32[start : start + rows, :] = gath[h, t].astype(jnp.float32)


def scatter_sum(part, half, send2, recv2, sems, mt, mh, nt):
    psend, precv, send, recv = sems
    rows = send2.shape[1]
    swap = remote(part.at[1 - mh], half, psend.at[0], precv.at[0], mt, 1 - mh)
    swap.start()
    swap.wait_recv()
    for t in range(nt):
        span = slice(t * rows, (t + 1) * rows)
        send2[t] = (part[mh, span, :] + half[span, :]).astype(jnp.bfloat16)
    copies = []
    for k in range(1, nt):
        peer = lax.rem(mt + k, nt)
        copy = remote(send2.at[peer], recv2.at[mt], send.at[k], recv.at[mt], peer, mh)
        copy.start()
        copies.append(copy)
    total = send2[mt].astype(jnp.float32)
    for k in range(1, nt):
        peer = lax.rem(mt + k, nt)
        remote(send2.at[peer], recv2.at[peer], send.at[k], recv.at[peer], peer, mh).wait_recv()
        total = total + recv2[peer].astype(jnp.float32)
    swap.wait_send()
    for copy in copies:
        copy.wait_send()
    return total


def front_kernel(nt, chunks, hid, gain, slots, wq, out, wbuf, gath, x32, acc, snd, rcv, wsem, gsem, asem):
    mt = lax.axis_index("tensor")
    mh = lax.axis_index("head")
    depth = wq.shape[1] // chunks
    cols = wq.shape[2]
    for c in range(chunks):
        span = pl.ds(c * depth, depth)
        pltpu.make_async_copy(wq.at[0, span, :], wbuf.at[span, :], wsem.at[c]).start()
    greet(mt, mh, nt)
    own = rms_scale(hid[...].astype(jnp.float32), gain[...]).astype(jnp.bfloat16)
    gather_rows(own, gath, x32, [gsem.at[i] for i in range(4)], mt, mh, nt)
    acc[...] = jnp.zeros_like(acc)

    @pl.loop(0, chunks)
    def _(c):
        span = pl.ds(pl.multiple_of(c * depth, depth), depth)
        pltpu.make_async_copy(wq.at[0, span, :], wbuf.at[span, :], wsem.at[c]).wait()
        acc[...] += jnp.dot(
            x32[:, span].astype(jnp.bfloat16), wbuf[span, :], preferred_element_type=jnp.float32
        )

    requests = x32.shape[0]
    pick = jnp.where(
        lax.broadcasted_iota(jnp.int32, (requests, requests), 0) == slots[...], 1.0, 0.0
    ).astype(jnp.bfloat16)
    acc[...] = jnp.dot(pick, acc[...].astype(jnp.bfloat16), preferred_element_type=jnp.float32)
    per = requests // nt
    for t in range(nt):
        snd[t] = acc[t * per : (t + 1) * per, :].astype(jnp.bfloat16)
    copies = []
    for k in range(1, nt):
        peer = lax.rem(mt + k, nt)
        copy = remote(snd.at[peer], rcv.at[mt], asem.at[0, k], asem.at[1, mt], peer, mh)
        copy.start()
        copies.append(copy)
    rcv[mt] = snd[mt]
    for k in range(1, nt):
        peer = lax.rem(mt + k, nt)
        remote(snd.at[peer], rcv.at[peer], asem.at[0, k], asem.at[1, peer], peer, mh).wait_recv()
    for t in range(nt):
        out[:, t * cols : (t + 1) * cols] = rcv[t]
    for copy in copies:
        copy.wait_send()


def dot_nt(lhs, rhs):
    return lax.dot_general(
        lhs, rhs, (((1,), (1,)), ((), ())), preferred_element_type=jnp.float32
    )


def back_kernel(
    nt, chunks, att, slots, hid, gain, wo, wg, wu, wd, out,
    wob, wgb, wub, wdb, rcv, ret, part, half, send2, recv2, gath, x32, gacc, uacc,
    wsem, asem, gsem, ssem,
):
    mt = lax.axis_index("tensor")
    mh = lax.axis_index("head")
    width = wo.shape[2]
    tile = width // chunks
    depth = wg.shape[1] // chunks

    def column_copy(src, dst, i, c):
        span = pl.ds(pl.multiple_of(c * tile, tile), tile)
        return pltpu.make_async_copy(src.at[:, span], dst.at[:, span], wsem.at[i, c])

    for c in range(chunks):
        column_copy(wo.at[0], wob, 0, c).start()
    for c in range(chunks):
        column_copy(wg, wgb, 1, c).start()
        column_copy(wu, wub, 2, c).start()
    for c in range(chunks):
        column_copy(wd, wdb, 3, c).start()
    greet(mt, mh, nt)
    copies = []
    for k in range(1, nt):
        peer = lax.rem(mt + k, nt)
        copy = remote(att.at[peer], rcv.at[mt], asem.at[0, k], asem.at[1, mt], peer, mh)
        copy.start()
        copies.append(copy)
    rcv[mt] = att[mt]
    for k in range(1, nt):
        peer = lax.rem(mt + k, nt)
        remote(att.at[peer], rcv.at[peer], asem.at[0, k], asem.at[1, peer], peer, mh).wait_recv()
    per = att.shape[1]
    for t in range(nt):
        ret[t * per : (t + 1) * per, :] = rcv[t].astype(jnp.float32)
    for copy in copies:
        copy.wait_send()
    requests = ret.shape[0]
    pick = jnp.where(
        lax.broadcasted_iota(jnp.int32, (requests, requests), 1) == slots[...], 1.0, 0.0
    ).astype(jnp.bfloat16)
    ret[...] = jnp.dot(pick, ret[...].astype(jnp.bfloat16), preferred_element_type=jnp.float32)
    middle_rows = requests // 2

    def column_dot(lhs, src, buf, i):
        @pl.loop(0, chunks)
        def _(c):
            column_copy(src, buf, i, c).wait()
            span = pl.ds(pl.multiple_of(c * tile, tile), tile)
            value = jnp.dot(lhs, buf[:, span], preferred_element_type=jnp.float32)
            part[0, :, span] = value[:middle_rows]
            part[1, :, span] = value[middle_rows:]

    column_dot(ret[...].astype(jnp.bfloat16), wo.at[0], wob, 0)
    summed = scatter_sum(
        part, half.at[0], send2.at[0], recv2.at[0], [ssem.at[0, i] for i in range(4)], mt, mh, nt
    )
    middle = (summed + hid[...].astype(jnp.float32)).astype(jnp.bfloat16)
    middle32 = middle.astype(jnp.float32)
    normed = rms_scale(middle32, gain[...]).astype(jnp.bfloat16)
    gather_rows(normed, gath, x32, [gsem.at[i] for i in range(4)], mt, mh, nt)
    gacc[...] = jnp.zeros_like(gacc)
    uacc[...] = jnp.zeros_like(uacc)

    @pl.loop(0, chunks)
    def _(c):
        span = pl.ds(pl.multiple_of(c * depth, depth), depth)
        rows = x32[:, span].astype(jnp.bfloat16)
        column_copy(wg, wgb, 1, c).wait()
        gacc[...] += dot_nt(rows, wgb[:, span])
        column_copy(wu, wub, 2, c).wait()
        uacc[...] += dot_nt(rows, wub[:, span])

    gate = gacc[...]
    activation = (gate / (1.0 + jnp.exp(-gate)) * uacc[...]).astype(jnp.bfloat16)
    gacc[...] = activation.astype(jnp.float32)
    column_dot(gacc[...].astype(jnp.bfloat16), wd, wdb, 3)
    summed = scatter_sum(
        part, half.at[1], send2.at[1], recv2.at[1], [ssem.at[1, i] for i in range(4)], mt, mh, nt
    )
    out[...] = (middle32 + summed).astype(jnp.bfloat16)


def front(nt, hidden_state, input_gain, slots_row, w_qkv):
    rows, width = hidden_state.shape
    requests = rows * nt * 2
    cols = w_qkv.shape[2]
    per = requests // nt
    chunks = 5
    vmem = pl.BlockSpec(memory_space=pltpu.VMEM)
    anyspace = pl.BlockSpec(memory_space=pl.ANY)
    dma = pltpu.SemaphoreType.DMA
    return pl.pallas_call(
        functools.partial(front_kernel, nt, chunks),
        out_shape=jax.ShapeDtypeStruct((per, cols * nt), jnp.bfloat16),
        in_specs=[vmem, vmem, vmem, anyspace],
        out_specs=vmem,
        scratch_shapes=[
            pltpu.VMEM((width, cols), jnp.bfloat16),
            pltpu.VMEM((2, nt, rows, width), jnp.bfloat16),
            pltpu.VMEM((requests, width), jnp.float32),
            pltpu.VMEM((requests, cols), jnp.float32),
            pltpu.VMEM((nt, per, cols), jnp.bfloat16),
            pltpu.VMEM((nt, per, cols), jnp.bfloat16),
            dma((chunks,)),
            dma((4, nt)),
            dma((2, nt)),
        ],
        compiler_params=pltpu.CompilerParams(
            collective_id=0, has_side_effects=True, vmem_limit_bytes=VMEM_LIMIT
        ),
    )(hidden_state, input_gain, slots_row, w_qkv)


def back(nt, attended, slots_column, hidden_state, middle_gain, w_out, w_gate, w_up, w_down):
    rows, width = hidden_state.shape
    requests = rows * nt * 2
    per = requests // nt
    cols = w_out.shape[1]
    units = w_gate.shape[1]
    chunks = 5
    vmem = pl.BlockSpec(memory_space=pltpu.VMEM)
    anyspace = pl.BlockSpec(memory_space=pl.ANY)
    dma = pltpu.SemaphoreType.DMA
    bf16, f32 = jnp.bfloat16, jnp.float32
    return pl.pallas_call(
        functools.partial(back_kernel, nt, chunks),
        out_shape=jax.ShapeDtypeStruct((rows, width), bf16),
        in_specs=[vmem] * 4 + [anyspace] * 4,
        out_specs=vmem,
        scratch_shapes=[
            pltpu.VMEM((cols, width), bf16),
            pltpu.VMEM((units, width), bf16),
            pltpu.VMEM((units, width), bf16),
            pltpu.VMEM((units, width), bf16),
            pltpu.VMEM((nt, per, cols), bf16),
            pltpu.VMEM((requests, cols), f32),
            pltpu.VMEM((2, requests // 2, width), f32),
            pltpu.VMEM((2, requests // 2, width), f32),
            pltpu.VMEM((2, nt, rows, width), bf16),
            pltpu.VMEM((2, nt, rows, width), bf16),
            pltpu.VMEM((2, nt, rows, width), bf16),
            pltpu.VMEM((requests, width), f32),
            pltpu.VMEM((requests, units), f32),
            pltpu.VMEM((requests, units), f32),
            dma((4, chunks)),
            dma((2, nt)),
            dma((4, nt)),
            dma((2, 4, nt)),
        ],
        compiler_params=pltpu.CompilerParams(
            collective_id=1, has_side_effects=True, vmem_limit_bytes=VMEM_LIMIT
        ),
    )(attended, slots_column, hidden_state, middle_gain, w_out, w_gate.T, w_up.T, w_down)


def kernels_fit(nt, nh, hidden_state, w_qkv, w_out, w_gate):
    width = hidden_state.shape[1]
    units = w_gate.shape[1]
    weight_bytes = 2 * width * (w_out.shape[1] + 3 * units)
    other_bytes = 2 * nt * hidden_state.shape[0] * width * 24
    return (
        nh == 2
        and w_qkv.shape[2] % 128 == 0
        and w_out.shape[1] % 128 == 0
        and width % 1280 == 0
        and units % 16 == 0
        and weight_bytes + other_bytes < VMEM_LIMIT
    )


def per_device(
    nt,
    nh,
    hidden_state,
    input_gain,
    w_qkv,
    query_gain,
    key_gain,
    slot_of,
    lengths,
    key_cache,
    value_cache,
    key_scale,
    value_scale,
    w_out,
    middle_gain,
    w_gate,
    w_up,
    w_down,
):
    rows_local = hidden_state.shape[0]
    requests = slot_of.shape[0]
    fused = kernels_fit(nt, nh, hidden_state, w_qkv, w_out, w_gate)
    if fused:
        slots_by_head = slot_of.reshape(nt, nh, rows_local).transpose(1, 0, 2)
        owned_rows = front(
            nt,
            hidden_state,
            input_gain.reshape(1, -1),
            slots_by_head.reshape(1, requests),
            w_qkv,
        )
    else:
        normed_in = rms_scale(hidden_state.astype(jnp.float32), input_gain).astype(jnp.bfloat16)
        qkv_weights = w_qkv[0]
        qkv_local = jnp.dot(
            lax.all_gather(normed_in, ("tensor", "head"), axis=0, tiled=True),
            qkv_weights,
            preferred_element_type=jnp.float32,
        ).astype(jnp.bfloat16)
        request_of = (
            jnp.zeros((requests,), jnp.int32).at[slot_of].set(jnp.arange(requests, dtype=jnp.int32))
        )
        qkv_slots = jnp.take(qkv_local, request_of, axis=0)
        owned_rows = lax.all_to_all(qkv_slots, "tensor", split_axis=0, concat_axis=1, tiled=True)
    slots_here = owned_rows.shape[0]
    kv_local = key_cache.shape[1]
    cache_len = key_cache.shape[2]
    head_dim = key_cache.shape[3]
    block_size = cache_len // key_scale.shape[2]
    group_size = owned_rows.shape[1] // (kv_local * head_dim) - 2
    grouped = owned_rows.reshape(slots_here, kv_local, group_size + 2, head_dim)
    queries = grouped[:, :, :group_size].astype(jnp.float32)
    keys_new = grouped[:, :, group_size].astype(jnp.float32)
    values_new = grouped[:, :, group_size + 1]
    query_rot = rotate(rms_scale(queries, query_gain), lengths[:, None, None]).astype(jnp.bfloat16)
    key_rot = rotate(rms_scale(keys_new, key_gain), lengths[:, None]).astype(jnp.bfloat16)
    new_kv = jnp.stack([key_rot, values_new], axis=1)
    inverse_root = 1.0 / math.sqrt(head_dim)
    own_scores = (
        jnp.einsum("rgih,rgh->rgi", query_rot, key_rot, preferred_element_type=jnp.float32)
        * inverse_root
    )
    value_expand = jnp.repeat(value_scale, block_size, axis=2)
    key_expand = jnp.repeat(key_scale, block_size, axis=2)
    positions = jnp.arange(cache_len, dtype=jnp.int32)
    live_mask = positions[None, None, None, :] < lengths[:, None, None, None]
    raw_scores = jnp.einsum(
        "rgih,rgph->rgip", query_rot, key_cache, preferred_element_type=jnp.float32
    )
    cache_scores = jnp.where(
        live_mask, raw_scores * key_expand[:, :, None, :] * inverse_root, -jnp.inf
    )
    cache_weights, own_weights = softmax_weights(cache_scores, own_scores, value_expand)
    mixed_sum = jnp.einsum(
        "rgip,rgph->rgih", cache_weights, value_cache, preferred_element_type=jnp.float32
    )
    mixed_sum = (
        mixed_sum
        + own_weights.astype(jnp.float32)[..., None] * values_new.astype(jnp.float32)[:, :, None, :]
    )
    attended = mixed_sum.astype(jnp.bfloat16).reshape(slots_here, kv_local * group_size * head_dim)
    if fused:
        blocks = attended.reshape(slots_here, nt, -1).transpose(1, 0, 2)
        layer_out = back(
            nt,
            blocks,
            slots_by_head.reshape(requests, 1),
            hidden_state,
            middle_gain.reshape(1, -1),
            w_out,
            w_gate,
            w_up,
            w_down,
        )
        return (layer_out, new_kv)
    returned = lax.all_to_all(attended, "tensor", split_axis=1, concat_axis=0, tiled=True)
    by_request = jnp.take(returned, slot_of, axis=0)
    out_weights = w_out[0]
    own_offset = lax.axis_index(("tensor", "head")) * rows_local
    partial_out = jnp.dot(by_request, out_weights, preferred_element_type=jnp.float32)
    own_rows = lax.dynamic_slice_in_dim(
        partial_out, own_offset, rows_local, 0
    ) + hidden_state.astype(jnp.float32)
    with_residual = lax.dynamic_update_slice_in_dim(partial_out, own_rows, own_offset, 0)
    summed = lax.psum(with_residual, ("tensor", "head"))
    middle_all = summed.astype(jnp.bfloat16)
    normed_mid = rms_scale(middle_all.astype(jnp.float32), middle_gain).astype(jnp.bfloat16)
    activation = gate_units(normed_mid, w_gate, w_up)
    middle = lax.dynamic_slice_in_dim(middle_all, own_offset, rows_local, 0)
    reduced = lax.psum_scatter(
        jnp.dot(activation, w_down, preferred_element_type=jnp.float32),
        ("tensor", "head"),
        scatter_dimension=0,
        tiled=True,
    )
    layer_out = (middle.astype(jnp.float32) + reduced).astype(jnp.bfloat16)
    return (layer_out, new_kv)


def solution(mesh):
    return jax.shard_map(
        functools.partial(per_device, mesh.shape["tensor"], mesh.shape["head"]),
        mesh=mesh,
        in_specs=(
            P(("groups", "tensor", "head"), None),
            P(),
            P("head", None, "tensor"),
            P(),
            P(),
            P("groups"),
            P(("groups", "tensor")),
            P(("groups", "tensor"), "head", None, None),
            P(("groups", "tensor"), "head", None, None),
            P(("groups", "tensor"), "head", None),
            P(("groups", "tensor"), "head", None),
            P("head", "tensor", None),
            P(),
            P(None, ("tensor", "head")),
            P(None, ("tensor", "head")),
            P(("tensor", "head"), None),
        ),
        out_specs=(
            P(("groups", "tensor", "head"), None),
            P(("groups", "tensor"), None, "head", None),
        ),
        check_vma=False,
    )
```

```python
import functools
import math

import jax
import jax.numpy as jnp
from jax import lax
from jax.experimental import pallas as pl
from jax.experimental.pallas import tpu as pltpu
from jax.sharding import PartitionSpec as P

EPSILON = 1e-06
THETA = 1000000.0


def rms_scale(values, gain_vector):
    mean_square = jnp.mean(values * values, axis=-1, keepdims=True)
    return values * lax.rsqrt(mean_square + EPSILON) * gain_vector


def rotate(values, positions):
    full_width = values.shape[-1]
    half_width = full_width // 2
    frequency = jnp.power(
        jnp.float32(THETA), -jnp.arange(half_width, dtype=jnp.float32) * 2.0 / full_width
    )
    angles = positions.astype(jnp.float32)[..., None] * frequency
    cosine = jnp.cos(angles)
    sine_part = jnp.sin(angles)
    lower_half = values[..., :half_width]
    upper_half = values[..., half_width:]
    return jnp.concatenate(
        [
            lower_half * cosine - upper_half * sine_part,
            upper_half * cosine + lower_half * sine_part,
        ],
        axis=-1,
    )


def gate_units(normed_rows, w_gate, w_up):
    gate_part = jnp.dot(normed_rows, w_gate, preferred_element_type=jnp.float32)
    up_part = jnp.dot(normed_rows, w_up, preferred_element_type=jnp.float32)
    return (jax.nn.silu(gate_part) * up_part).astype(jnp.bfloat16)


def softmax_weights(cache_scores, own_scores, value_expand):
    highest = jnp.maximum(jnp.max(cache_scores, axis=-1), own_scores)
    cache_exp = jnp.exp(cache_scores - highest[..., None])
    own_exp = jnp.exp(own_scores - highest)
    denominator = jnp.sum(cache_exp, axis=-1) + own_exp
    cache_weights = (cache_exp * value_expand[:, :, None, :] / denominator[..., None]).astype(
        jnp.bfloat16
    )
    own_weights = (own_exp / denominator).astype(jnp.bfloat16)
    return (cache_weights, own_weights)


MESH_ID = pl.DeviceIdType.MESH
VMEM_LIMIT = 66_500_000


def remote(src, dst, send_sem, recv_sem, tensor_index, head_index):
    return pltpu.make_async_remote_copy(
        src_ref=src,
        dst_ref=dst,
        send_sem=send_sem,
        recv_sem=recv_sem,
        device_id={"tensor": tensor_index, "head": head_index},
        device_id_type=MESH_ID,
    )


def greet(mt, mh, nt):
    barrier = pltpu.get_barrier_semaphore()
    for k in range(1, nt):
        pl.semaphore_signal(
            barrier,
            inc=1,
            device_id={"tensor": lax.rem(mt + k, nt), "head": mh},
            device_id_type=MESH_ID,
        )
    pl.semaphore_signal(
        barrier, inc=1, device_id={"tensor": mt, "head": 1 - mh}, device_id_type=MESH_ID
    )
    pl.semaphore_wait(barrier, nt)


def gather_rows(own, gath, part, sems, mt, mh, nt):
    send, recv, fsend, frecv = sems
    rows = own.shape[0]
    chunks, tile = part.shape[0], part.shape[3]
    gath[mh, mt] = own
    copies = []
    for k in range(1, nt):
        copy = remote(
            gath.at[mh, mt], gath.at[mh, mt], send.at[k], recv.at[mt], lax.rem(mt + k, nt), mh
        )
        copy.start()
        copies.append(copy)
    copy = remote(gath.at[mh, mt], gath.at[mh, mt], fsend.at[mt], frecv.at[mt], mt, 1 - mh)
    copy.start()
    copies.append(copy)
    for k in range(1, nt):
        peer = lax.rem(mt + k, nt)
        block = gath.at[mh, peer]
        remote(block, block, send.at[k], recv.at[peer], mt, 1 - mh).wait_recv()
        copy = remote(block, block, fsend.at[peer], frecv.at[peer], mt, 1 - mh)
        copy.start()
        copies.append(copy)
    for t in range(nt):
        block = gath.at[1 - mh, t]
        remote(block, block, fsend.at[t], frecv.at[t], mt, 1 - mh).wait_recv()
    for copy in copies:
        copy.wait_send()
    for h in range(2):
        for t in range(nt):
            values = gath[h, t].astype(jnp.float32)
            for c in range(chunks):
                part[c, h, t * rows : (t + 1) * rows, :] = values[:, c * tile : (c + 1) * tile]


def matmul_scatter(product, part, half, send2, recv2, total, sems, mt, mh, nt):
    psend, precv, send, recv = sems
    chunks, tile = part.shape[0], part.shape[3]
    lines = part.shape[2]
    rows = send2.shape[2]

    def swap(c):
        return remote(part.at[c, 1 - mh], half.at[c], psend.at[c], precv.at[c], mt, 1 - mh)

    def spread(c, k):
        peer = lax.rem(mt + k, nt)
        return remote(
            send2.at[c, peer], recv2.at[c, mt], send.at[c, k], recv.at[c, mt], peer, mh
        )

    @pl.loop(0, chunks + 1)
    def _(step):
        @pl.when(step < chunks)
        def _():
            value = product(step)
            part[step, 0] = value[:lines]
            part[step, 1] = value[lines:]
            swap(step).start()

        @pl.when(step > 0)
        def _():
            c = step - 1
            swap(c).wait_recv()
            for t in range(nt):
                span = slice(t * rows, (t + 1) * rows)
                send2[c, t] = (part[c, mh, span, :] + half[c, span, :]).astype(jnp.bfloat16)
            for k in range(1, nt):
                spread(c, k).start()

    for c in range(chunks):
        value = send2[c, mt].astype(jnp.float32)
        for k in range(1, nt):
            peer = lax.rem(mt + k, nt)
            block = recv2.at[c, peer]
            remote(block, block, send.at[c, k], recv.at[c, peer], peer, mh).wait_recv()
            value = value + recv2[c, peer].astype(jnp.float32)
        total[:, c * tile : (c + 1) * tile] = value

    @pl.loop(0, chunks)
    def _(c):
        swap(c).wait_send()
        for k in range(1, nt):
            spread(c, k).wait_send()


def exchange(snd, rcv, sems, mt, mh, nt):
    copies = []
    for k in range(1, nt):
        peer = lax.rem(mt + k, nt)
        copy = remote(snd.at[peer], rcv.at[mt], sems.at[0, k], sems.at[1, mt], peer, mh)
        copy.start()
        copies.append(copy)
    rcv[mt] = snd[mt]
    for k in range(1, nt):
        peer = lax.rem(mt + k, nt)
        block = rcv.at[peer]
        remote(block, block, sems.at[0, k], sems.at[1, peer], peer, mh).wait_recv()
    for copy in copies:
        copy.wait_send()


def dot_nt(lhs, rhs):
    return lax.dot_general(
        lhs, rhs, (((1,), (1,)), ((), ())), preferred_element_type=jnp.float32
    )


def turn(values, cosine, sine):
    return values * cosine + pltpu.roll(values, values.shape[-1] // 2, values.ndim - 1) * sine


def scale_row(scales, s, g, block_size, blocks):
    lane = lax.broadcasted_iota(jnp.int32, (1, block_size * blocks), 1)
    row = jnp.full(lane.shape, scales[s, g, 0], jnp.float32)
    for b in range(1, blocks):
        row = jnp.where(lane >= b * block_size, scales[s, g, b], row)
    return row


def attend(rcv, grid, newkv, asnd, kbuf, vbuf, lens, kscale, vscale, qgain, kgain, cosine, sine):
    nt, slots_here, cols = rcv.shape
    kv_local, cache_len, head_dim = kbuf.shape[1:]
    blocks = kscale.shape[2]
    per_source = cols // head_dim
    span = per_source * nt // kv_local
    group = span - 2
    share = asnd.shape[2]
    inverse_root = 1.0 / math.sqrt(head_dim)
    for t in range(nt):
        values = rcv[t].astype(jnp.float32)
        for c in range(per_source):
            g, r = divmod(t * per_source + c, span)
            for s in range(slots_here):
                grid[s * kv_local + g, r : r + 1, :] = values[
                    s : s + 1, c * head_dim : (c + 1) * head_dim
                ]
    lane = lax.broadcasted_iota(jnp.int32, (1, cache_len), 1)
    for s in range(slots_here):
        live = lane < lens[s]
        cos_row, sin_row = cosine[s : s + 1, :], sine[s : s + 1, :]
        for g in range(kv_local):
            at = s * kv_local + g
            query = turn(rms_scale(grid[at, 0:group, :], qgain[...]), cos_row, sin_row)
            key = turn(rms_scale(grid[at, group : group + 1, :], kgain[...]), cos_row, sin_row)
            query = query.astype(jnp.bfloat16)
            key = key.astype(jnp.bfloat16).astype(jnp.float32)
            value = grid[at, group + 1 : group + 2, :]
            newkv[s, 0, g : g + 1, :] = key
            newkv[s, 1, g : g + 1, :] = value
            own = (
                jnp.sum(query.astype(jnp.float32) * key, axis=1, keepdims=True) * inverse_root
            )
            raw = dot_nt(query, kbuf[s, g])
            key_row = scale_row(kscale, s, g, cache_len // blocks, blocks)
            value_row = scale_row(vscale, s, g, cache_len // blocks, blocks)
            scores = jnp.where(live, raw * key_row * inverse_root, -jnp.inf)
            top = jnp.maximum(jnp.max(scores, axis=1, keepdims=True), own)
            exps = jnp.exp(scores - top)
            own_exp = jnp.exp(own - top)
            denominator = jnp.sum(exps, axis=1, keepdims=True) + own_exp
            weights = (exps * value_row / denominator).astype(jnp.bfloat16)
            own_weight = (own_exp / denominator).astype(jnp.bfloat16).astype(jnp.float32)
            mixed = jnp.dot(weights, vbuf[s, g], preferred_element_type=jnp.float32)
            mixed = mixed + own_weight * value
            for j in range(group // share):
                asnd[(g * group) // share + j, s] = mixed[j * share : (j + 1) * share].astype(
                    jnp.bfloat16
                )


def layer_kernel(
    nt, hid, gain, slots, qgain, kgain, lens, kscale, vscale, cosine, sine, mgain,
    wq, kc, vc, wo, wg, wu, wd, out, kvout,
    wqb, kb, vb, wob, wgb, wub, wdb, gath, part, half, send2, recv2, total, acc, snd, rcv,
    grid, newkv, asnd, arcv, heads, gacc, uacc, wsem, bsem, asem, gsem, psem, ssem,
):
    mt = lax.axis_index("tensor")
    mh = lax.axis_index("head")
    chunks, tile = part.shape[0], part.shape[3]
    keep = wdb.shape[0]
    spare = wd.shape[0] - keep
    requests = acc.shape[0]

    def rows_of(c):
        span = pl.ds(pl.multiple_of(c * tile, tile), tile)
        return pltpu.make_async_copy(wq.at[0, span, :], wqb.at[span, :], wsem.at[0, c])

    def columns_of(src, dst, i, c):
        span = pl.ds(pl.multiple_of(c * tile, tile), tile)
        return pltpu.make_async_copy(src.at[:, span], dst.at[:, span], wsem.at[i, c])

    down = wd.at[pl.ds(0, keep), :]
    tail = pltpu.make_async_copy(
        wd.at[pl.ds(keep, spare), :], wob.at[pl.ds(0, spare), :], bsem.at[2]
    )
    key_copy = pltpu.make_async_copy(kc, kb, bsem.at[0])
    value_copy = pltpu.make_async_copy(vc, vb, bsem.at[1])
    for c in range(chunks):
        rows_of(c).start()
    key_copy.start()
    value_copy.start()
    for c in range(chunks):
        columns_of(wo.at[0], wob, 1, c).start()
    greet(mt, mh, nt)
    own = rms_scale(hid[...].astype(jnp.float32), gain[...]).astype(jnp.bfloat16)
    gather_rows(own, gath, part, [gsem.at[0, i] for i in range(4)], mt, mh, nt)
    for c in range(chunks):
        columns_of(wg, wgb, 2, c).start()
        columns_of(wu, wub, 3, c).start()
    acc[...] = jnp.zeros_like(acc)

    def gathered(c):
        return part[c].reshape(requests, tile).astype(jnp.bfloat16)

    @pl.loop(0, chunks)
    def _(c):
        span = pl.ds(pl.multiple_of(c * tile, tile), tile)
        rows_of(c).wait()
        acc[...] += jnp.dot(gathered(c), wqb[span, :], preferred_element_type=jnp.float32)

    shape = (requests, requests)
    down_iota = lax.broadcasted_iota(jnp.int32, shape, 0)
    across = lax.broadcasted_iota(jnp.int32, shape, 1)
    rows = hid.shape[0]
    half_lines = requests // 2
    request_at = (
        lax.div(lax.rem(across, half_lines), rows) * (2 * rows)
        + lax.div(across, half_lines) * rows
        + lax.rem(across, rows)
    )
    place = jnp.where(down_iota == request_at, 1.0, 0.0).astype(jnp.bfloat16)
    by_slot = jnp.where(down_iota == slots[...], 1.0, 0.0).astype(jnp.bfloat16)
    pick = jnp.dot(by_slot, place, preferred_element_type=jnp.float32).astype(jnp.bfloat16)
    acc[...] = jnp.dot(pick, acc[...].astype(jnp.bfloat16), preferred_element_type=jnp.float32)
    per = requests // nt
    for t in range(nt):
        snd[t] = acc[t * per : (t + 1) * per, :].astype(jnp.bfloat16)
    exchange(snd, rcv, asem.at[0], mt, mh, nt)
    for c in range(chunks):
        columns_of(down, wdb, 4, c).start()
    key_copy.wait()
    value_copy.wait()
    attend(
        rcv, grid, newkv, asnd, kb, vb, lens, kscale, vscale, qgain, kgain, cosine, sine
    )
    exchange(asnd, arcv, asem.at[1], mt, mh, nt)
    kvout[...] = newkv[...].astype(jnp.bfloat16)
    share, head_dim = asnd.shape[2], asnd.shape[3]
    for t in range(nt):
        for s in range(per):
            values = arcv[t, s].astype(jnp.float32)
            for j in range(share):
                heads[t * per + s : t * per + s + 1, j * head_dim : (j + 1) * head_dim] = values[
                    j : j + 1, :
                ]
    attended = lax.dot_general(
        pick,
        heads[...].astype(jnp.bfloat16),
        (((0,), (0,)), ((), ())),
        preferred_element_type=jnp.float32,
    ).astype(jnp.bfloat16)

    def project(c):
        span = pl.ds(pl.multiple_of(c * tile, tile), tile)
        columns_of(wo.at[0], wob, 1, c).wait()
        return jnp.dot(attended, wob[:, span], preferred_element_type=jnp.float32)

    matmul_scatter(
        project, part, half, send2, recv2, total,
        [psem.at[0, 0], psem.at[0, 1], ssem.at[0, 0], ssem.at[0, 1]], mt, mh, nt,
    )
    tail.start()
    middle = (total[...] + hid[...].astype(jnp.float32)).astype(jnp.bfloat16).astype(jnp.float32)
    normed = rms_scale(middle, mgain[...]).astype(jnp.bfloat16)
    gather_rows(normed, gath, part, [gsem.at[1, i] for i in range(4)], mt, mh, nt)
    gacc[...] = jnp.zeros_like(gacc)
    uacc[...] = jnp.zeros_like(uacc)

    @pl.loop(0, chunks)
    def _(c):
        span = pl.ds(pl.multiple_of(c * tile, tile), tile)
        lhs = gathered(c)
        columns_of(wg, wgb, 2, c).wait()
        gacc[...] += dot_nt(lhs, wgb[:, span])
        columns_of(wu, wub, 3, c).wait()
        uacc[...] += dot_nt(lhs, wub[:, span])

    gate = gacc[...]
    gacc[...] = gate / (1.0 + jnp.exp(-gate)) * uacc[...]
    active = gacc[...].astype(jnp.bfloat16)
    tail.wait()

    def lower(c):
        span = pl.ds(pl.multiple_of(c * tile, tile), tile)
        columns_of(down, wdb, 4, c).wait()
        return jnp.dot(
            active[:, :keep], wdb[:, span], preferred_element_type=jnp.float32
        ) + jnp.dot(active[:, keep:], wob[:spare, span], preferred_element_type=jnp.float32)

    matmul_scatter(
        lower, part, half, send2, recv2, total,
        [psem.at[1, 0], psem.at[1, 1], ssem.at[1, 0], ssem.at[1, 1]], mt, mh, nt,
    )
    out[...] = (middle + total[...]).astype(jnp.bfloat16)


def kept_rows(w_out, w_down):
    return -(-(w_down.shape[0] - w_out.shape[1]) // 128) * 128


def fused_layer(
    nt, hidden_state, input_gain, w_qkv, query_gain, key_gain, slot_of, lengths, key_cache,
    value_cache, key_scale, value_scale, w_out, middle_gain, w_gate, w_up, w_down,
):
    rows, width = hidden_state.shape
    requests = rows * nt * 2
    cols = w_qkv.shape[2]
    per = requests // nt
    chunks = 5
    tile = width // chunks
    units = w_gate.shape[1]
    kv_local, head_dim = key_cache.shape[1], key_cache.shape[3]
    group = cols * nt // (kv_local * head_dim) - 2
    share = kv_local * group // nt
    keep = kept_rows(w_out, w_down)
    frequency = jnp.power(
        jnp.float32(THETA), -jnp.arange(head_dim // 2, dtype=jnp.float32) * 2.0 / head_dim
    )
    angles = lengths.astype(jnp.float32)[:, None] * frequency
    cosine, sine = jnp.cos(angles), jnp.sin(angles)
    cosine = jnp.concatenate([cosine, cosine], axis=1)
    sine = jnp.concatenate([-sine, sine], axis=1)
    vmem = pl.BlockSpec(memory_space=pltpu.VMEM)
    smem = pl.BlockSpec(memory_space=pltpu.SMEM)
    anyspace = pl.BlockSpec(memory_space=pl.ANY)
    dma = pltpu.SemaphoreType.DMA
    bf16, f32 = jnp.bfloat16, jnp.float32
    line = lambda a: a.reshape(1, -1)
    return pl.pallas_call(
        functools.partial(layer_kernel, nt),
        out_shape=(
            jax.ShapeDtypeStruct((rows, width), bf16),
            jax.ShapeDtypeStruct((per, 2, kv_local, head_dim), bf16),
        ),
        in_specs=[vmem] * 5 + [smem] * 3 + [vmem] * 3 + [anyspace] * 7,
        out_specs=(vmem, vmem),
        scratch_shapes=[
            pltpu.VMEM((width, cols), bf16),
            pltpu.VMEM(key_cache.shape, bf16),
            pltpu.VMEM(value_cache.shape, bf16),
            pltpu.VMEM((w_out.shape[1], width), bf16),
            pltpu.VMEM((units, width), bf16),
            pltpu.VMEM((units, width), bf16),
            pltpu.VMEM((keep, width), bf16),
            pltpu.VMEM((2, nt, rows, width), bf16),
            pltpu.VMEM((chunks, 2, requests // 2, tile), f32),
            pltpu.VMEM((chunks, requests // 2, tile), f32),
            pltpu.VMEM((chunks, nt, rows, tile), bf16),
            pltpu.VMEM((chunks, nt, rows, tile), bf16),
            pltpu.VMEM((rows, width), f32),
            pltpu.VMEM((requests, cols), f32),
            pltpu.VMEM((nt, per, cols), bf16),
            pltpu.VMEM((nt, per, cols), bf16),
            pltpu.VMEM((per * kv_local, 16, head_dim), f32),
            pltpu.VMEM((per, 2, kv_local, head_dim), f32),
            pltpu.VMEM((nt, per, share, head_dim), bf16),
            pltpu.VMEM((nt, per, share, head_dim), bf16),
            pltpu.VMEM((requests, w_out.shape[1]), f32),
            pltpu.VMEM((requests, units), f32),
            pltpu.VMEM((requests, units), f32),
            dma((5, chunks)),
            dma((3,)),
            dma((2, 2, nt)),
            dma((2, 4, nt)),
            dma((2, 2, chunks)),
            dma((2, 2, chunks, nt)),
        ],
        compiler_params=pltpu.CompilerParams(
            collective_id=0, has_side_effects=True, vmem_limit_bytes=VMEM_LIMIT
        ),
    )(
        hidden_state, line(input_gain), line(slot_of), line(query_gain), line(key_gain),
        lengths, key_scale, value_scale, cosine, sine, line(middle_gain),
        w_qkv, key_cache, value_cache, w_out, w_gate.T, w_up.T, w_down,
    )


def kernels_fit(nt, nh, hidden_state, w_qkv, key_cache, w_out, w_gate, w_down):
    width = hidden_state.shape[1]
    kv_local, head_dim = key_cache.shape[1], key_cache.shape[3]
    cols = w_qkv.shape[2]
    if nh != 2 or head_dim != 128 or cols % head_dim or w_out.shape[1] % head_dim:
        return False
    if width % 640 or w_gate.shape[1] % 16 or cols * nt % (kv_local * head_dim):
        return False
    group = cols * nt // (kv_local * head_dim) - 2
    share = kv_local * group // nt
    if group != 8 or share == 0 or group % share:
        return False
    keep = kept_rows(w_out, w_down)
    if not 0 < keep < w_down.shape[0]:
        return False
    weights = width * (cols + w_out.shape[1] + 2 * w_gate.shape[1] + keep)
    caches = 2 * math.prod(key_cache.shape)
    others = 2 * nt * hidden_state.shape[0] * width * 14
    return 2 * (weights + caches) + others < VMEM_LIMIT


def per_device(
    nt,
    nh,
    hidden_state,
    input_gain,
    w_qkv,
    query_gain,
    key_gain,
    slot_of,
    lengths,
    key_cache,
    value_cache,
    key_scale,
    value_scale,
    w_out,
    middle_gain,
    w_gate,
    w_up,
    w_down,
):
    rows_local = hidden_state.shape[0]
    requests = slot_of.shape[0]
    if kernels_fit(nt, nh, hidden_state, w_qkv, key_cache, w_out, w_gate, w_down):
        return fused_layer(
            nt, hidden_state, input_gain, w_qkv, query_gain, key_gain, slot_of, lengths,
            key_cache, value_cache, key_scale, value_scale, w_out, middle_gain, w_gate, w_up,
            w_down,
        )
    normed_in = rms_scale(hidden_state.astype(jnp.float32), input_gain).astype(jnp.bfloat16)
    qkv_weights = w_qkv[0]
    qkv_local = jnp.dot(
        lax.all_gather(normed_in, ("tensor", "head"), axis=0, tiled=True),
        qkv_weights,
        preferred_element_type=jnp.float32,
    ).astype(jnp.bfloat16)
    request_of = (
        jnp.zeros((requests,), jnp.int32).at[slot_of].set(jnp.arange(requests, dtype=jnp.int32))
    )
    qkv_slots = jnp.take(qkv_local, request_of, axis=0)
    owned_rows = lax.all_to_all(qkv_slots, "tensor", split_axis=0, concat_axis=1, tiled=True)
    slots_here = owned_rows.shape[0]
    kv_local = key_cache.shape[1]
    cache_len = key_cache.shape[2]
    head_dim = key_cache.shape[3]
    block_size = cache_len // key_scale.shape[2]
    group_size = owned_rows.shape[1] // (kv_local * head_dim) - 2
    grouped = owned_rows.reshape(slots_here, kv_local, group_size + 2, head_dim)
    queries = grouped[:, :, :group_size].astype(jnp.float32)
    keys_new = grouped[:, :, group_size].astype(jnp.float32)
    values_new = grouped[:, :, group_size + 1]
    query_rot = rotate(rms_scale(queries, query_gain), lengths[:, None, None]).astype(jnp.bfloat16)
    key_rot = rotate(rms_scale(keys_new, key_gain), lengths[:, None]).astype(jnp.bfloat16)
    new_kv = jnp.stack([key_rot, values_new], axis=1)
    inverse_root = 1.0 / math.sqrt(head_dim)
    own_scores = (
        jnp.einsum("rgih,rgh->rgi", query_rot, key_rot, preferred_element_type=jnp.float32)
        * inverse_root
    )
    value_expand = jnp.repeat(value_scale, block_size, axis=2)
    key_expand = jnp.repeat(key_scale, block_size, axis=2)
    positions = jnp.arange(cache_len, dtype=jnp.int32)
    live_mask = positions[None, None, None, :] < lengths[:, None, None, None]
    raw_scores = jnp.einsum(
        "rgih,rgph->rgip", query_rot, key_cache, preferred_element_type=jnp.float32
    )
    cache_scores = jnp.where(
        live_mask, raw_scores * key_expand[:, :, None, :] * inverse_root, -jnp.inf
    )
    cache_weights, own_weights = softmax_weights(cache_scores, own_scores, value_expand)
    mixed_sum = jnp.einsum(
        "rgip,rgph->rgih", cache_weights, value_cache, preferred_element_type=jnp.float32
    )
    mixed_sum = (
        mixed_sum
        + own_weights.astype(jnp.float32)[..., None] * values_new.astype(jnp.float32)[:, :, None, :]
    )
    attended = mixed_sum.astype(jnp.bfloat16).reshape(slots_here, kv_local * group_size * head_dim)
    returned = lax.all_to_all(attended, "tensor", split_axis=1, concat_axis=0, tiled=True)
    by_request = jnp.take(returned, slot_of, axis=0)
    out_weights = w_out[0]
    own_offset = lax.axis_index(("tensor", "head")) * rows_local
    partial_out = jnp.dot(by_request, out_weights, preferred_element_type=jnp.float32)
    own_rows = lax.dynamic_slice_in_dim(
        partial_out, own_offset, rows_local, 0
    ) + hidden_state.astype(jnp.float32)
    with_residual = lax.dynamic_update_slice_in_dim(partial_out, own_rows, own_offset, 0)
    summed = lax.psum(with_residual, ("tensor", "head"))
    middle_all = summed.astype(jnp.bfloat16)
    normed_mid = rms_scale(middle_all.astype(jnp.float32), middle_gain).astype(jnp.bfloat16)
    activation = gate_units(normed_mid, w_gate, w_up)
    middle = lax.dynamic_slice_in_dim(middle_all, own_offset, rows_local, 0)
    reduced = lax.psum_scatter(
        jnp.dot(activation, w_down, preferred_element_type=jnp.float32),
        ("tensor", "head"),
        scatter_dimension=0,
        tiled=True,
    )
    layer_out = (middle.astype(jnp.float32) + reduced).astype(jnp.bfloat16)
    return (layer_out, new_kv)


def solution(mesh):
    return jax.shard_map(
        functools.partial(per_device, mesh.shape["tensor"], mesh.shape["head"]),
        mesh=mesh,
        in_specs=(
            P(("groups", "tensor", "head"), None),
            P(),
            P("head", None, "tensor"),
            P(),
            P(),
            P("groups"),
            P(("groups", "tensor")),
            P(("groups", "tensor"), "head", None, None),
            P(("groups", "tensor"), "head", None, None),
            P(("groups", "tensor"), "head", None),
            P(("groups", "tensor"), "head", None),
            P("head", "tensor", None),
            P(),
            P(None, ("tensor", "head")),
            P(None, ("tensor", "head")),
            P(("tensor", "head"), None),
        ),
        out_specs=(
            P(("groups", "tensor", "head"), None),
            P(("groups", "tensor"), None, "head", None),
        ),
        check_vma=False,
    )
```

```python
import functools
import math

import jax
import jax.numpy as jnp
from jax import lax
from jax.experimental import pallas as pl
from jax.experimental.pallas import tpu as pltpu
from jax.sharding import PartitionSpec as P

EPSILON = 1e-06
THETA = 1000000.0


def rms_scale(values, gain_vector):
    mean_square = jnp.mean(values * values, axis=-1, keepdims=True)
    return values * lax.rsqrt(mean_square + EPSILON) * gain_vector


def rotate(values, positions):
    full_width = values.shape[-1]
    half_width = full_width // 2
    frequency = jnp.power(
        jnp.float32(THETA), -jnp.arange(half_width, dtype=jnp.float32) * 2.0 / full_width
    )
    angles = positions.astype(jnp.float32)[..., None] * frequency
    cosine = jnp.cos(angles)
    sine_part = jnp.sin(angles)
    lower_half = values[..., :half_width]
    upper_half = values[..., half_width:]
    return jnp.concatenate(
        [
            lower_half * cosine - upper_half * sine_part,
            upper_half * cosine + lower_half * sine_part,
        ],
        axis=-1,
    )


def gate_units(normed_rows, w_gate, w_up):
    gate_part = jnp.dot(normed_rows, w_gate, preferred_element_type=jnp.float32)
    up_part = jnp.dot(normed_rows, w_up, preferred_element_type=jnp.float32)
    return (jax.nn.silu(gate_part) * up_part).astype(jnp.bfloat16)


def softmax_weights(cache_scores, own_scores, value_expand):
    highest = jnp.maximum(jnp.max(cache_scores, axis=-1), own_scores)
    cache_exp = jnp.exp(cache_scores - highest[..., None])
    own_exp = jnp.exp(own_scores - highest)
    denominator = jnp.sum(cache_exp, axis=-1) + own_exp
    cache_weights = (cache_exp * value_expand[:, :, None, :] / denominator[..., None]).astype(
        jnp.bfloat16
    )
    own_weights = (own_exp / denominator).astype(jnp.bfloat16)
    return (cache_weights, own_weights)


MESH_ID = pl.DeviceIdType.MESH
VMEM_LIMIT = 66_500_000


def remote(src, dst, send_sem, recv_sem, tensor_index, head_index):
    return pltpu.make_async_remote_copy(
        src_ref=src,
        dst_ref=dst,
        send_sem=send_sem,
        recv_sem=recv_sem,
        device_id={"tensor": tensor_index, "head": head_index},
        device_id_type=MESH_ID,
    )


def greet(mt, mh, nt):
    barrier = pltpu.get_barrier_semaphore()
    for k in range(1, nt):
        pl.semaphore_signal(
            barrier,
            inc=1,
            device_id={"tensor": lax.rem(mt + k, nt), "head": mh},
            device_id_type=MESH_ID,
        )
    pl.semaphore_signal(
        barrier, inc=1, device_id={"tensor": mt, "head": 1 - mh}, device_id_type=MESH_ID
    )
    pl.semaphore_wait(barrier, nt)


def gather_rows(own, gath, part, sems, mt, mh, nt):
    send, recv, fsend, frecv = sems
    rows = own.shape[0]
    chunks, tile = part.shape[0], part.shape[3]
    gath[mh, mt] = own
    copies = []
    for k in range(1, nt):
        copy = remote(
            gath.at[mh, mt], gath.at[mh, mt], send.at[k], recv.at[mt], lax.rem(mt + k, nt), mh
        )
        copy.start()
        copies.append(copy)
    copy = remote(gath.at[mh, mt], gath.at[mh, mt], fsend.at[mt], frecv.at[mt], mt, 1 - mh)
    copy.start()
    copies.append(copy)
    for k in range(1, nt):
        peer = lax.rem(mt + k, nt)
        block = gath.at[mh, peer]
        remote(block, block, send.at[k], recv.at[peer], mt, 1 - mh).wait_recv()
        copy = remote(block, block, fsend.at[peer], frecv.at[peer], mt, 1 - mh)
        copy.start()
        copies.append(copy)
    for t in range(nt):
        block = gath.at[1 - mh, t]
        remote(block, block, fsend.at[t], frecv.at[t], mt, 1 - mh).wait_recv()
    for copy in copies:
        copy.wait_send()
    for h in range(2):
        for t in range(nt):
            values = gath[h, t].astype(jnp.float32)
            for c in range(chunks):
                part[c, h, t * rows : (t + 1) * rows, :] = values[:, c * tile : (c + 1) * tile]


def matmul_scatter(product, part, half, send2, recv2, total, sems, mt, mh, nt):
    psend, precv, send, recv = sems
    chunks, tile = part.shape[0], part.shape[3]
    lines = part.shape[2]
    rows = send2.shape[2]

    def swap(c):
        return remote(part.at[c, 1 - mh], half.at[c], psend.at[c], precv.at[c], mt, 1 - mh)

    def spread(c, k):
        peer = lax.rem(mt + k, nt)
        return remote(
            send2.at[c, peer], recv2.at[c, mt], send.at[c, k], recv.at[c, mt], peer, mh
        )

    @pl.loop(0, chunks + 1)
    def _(step):
        @pl.when(step < chunks)
        def _():
            value = product(step)
            part[step, 0] = value[:lines]
            part[step, 1] = value[lines:]
            swap(step).start()

        @pl.when(step > 0)
        def _():
            c = step - 1
            swap(c).wait_recv()
            for t in range(nt):
                span = slice(t * rows, (t + 1) * rows)
                send2[c, t] = (part[c, mh, span, :] + half[c, span, :]).astype(jnp.bfloat16)
            for k in range(1, nt):
                spread(c, k).start()

    for c in range(chunks):
        value = send2[c, mt].astype(jnp.float32)
        for k in range(1, nt):
            peer = lax.rem(mt + k, nt)
            block = recv2.at[c, peer]
            remote(block, block, send.at[c, k], recv.at[c, peer], peer, mh).wait_recv()
            value = value + recv2[c, peer].astype(jnp.float32)
        total[:, c * tile : (c + 1) * tile] = value

    @pl.loop(0, chunks)
    def _(c):
        swap(c).wait_send()
        for k in range(1, nt):
            spread(c, k).wait_send()


def exchange(snd, rcv, sems, mt, mh, nt):
    copies = []
    for k in range(1, nt):
        peer = lax.rem(mt + k, nt)
        copy = remote(snd.at[peer], rcv.at[mt], sems.at[0, k], sems.at[1, mt], peer, mh)
        copy.start()
        copies.append(copy)
    rcv[mt] = snd[mt]
    for k in range(1, nt):
        peer = lax.rem(mt + k, nt)
        block = rcv.at[peer]
        remote(block, block, sems.at[0, k], sems.at[1, peer], peer, mh).wait_recv()
    for copy in copies:
        copy.wait_send()


def dot_nt(lhs, rhs):
    return lax.dot_general(
        lhs, rhs, (((1,), (1,)), ((), ())), preferred_element_type=jnp.float32
    )


def turn(values, cosine, sine):
    return values * cosine + pltpu.roll(values, values.shape[-1] // 2, values.ndim - 1) * sine


def scale_row(scales, s, g, block_size, blocks):
    lane = lax.broadcasted_iota(jnp.int32, (1, block_size * blocks), 1)
    row = jnp.full(lane.shape, scales[0, s, g], jnp.float32)
    for b in range(1, blocks):
        row = jnp.where(lane >= b * block_size, scales[b, s, g], row)
    return row


def attend(rcv, grid, newkv, asnd, kbuf, vbuf, lens, kscale, vscale, qgain, kgain, cosine, sine):
    nt, slots_here, cols = rcv.shape
    kv_local, cache_len, head_dim = kbuf.shape[1:]
    blocks = kscale.shape[0]
    per_source = cols // head_dim
    span = per_source * nt // kv_local
    group = span - 2
    share = asnd.shape[2]
    inverse_root = 1.0 / math.sqrt(head_dim)
    for t in range(nt):
        values = rcv[t].astype(jnp.float32)
        for c in range(per_source):
            g, r = divmod(t * per_source + c, span)
            for s in range(slots_here):
                grid[s * kv_local + g, r : r + 1, :] = values[
                    s : s + 1, c * head_dim : (c + 1) * head_dim
                ]
    lane = lax.broadcasted_iota(jnp.int32, (1, cache_len), 1)
    for s in range(slots_here):
        live = lane < lens[s]
        cos_row, sin_row = cosine[s : s + 1, :], sine[s : s + 1, :]
        for g in range(kv_local):
            at = s * kv_local + g
            query = turn(rms_scale(grid[at, 0:group, :], qgain[...]), cos_row, sin_row)
            key = turn(rms_scale(grid[at, group : group + 1, :], kgain[...]), cos_row, sin_row)
            query = query.astype(jnp.bfloat16)
            key = key.astype(jnp.bfloat16).astype(jnp.float32)
            value = grid[at, group + 1 : group + 2, :]
            newkv[s, 0, g : g + 1, :] = key
            newkv[s, 1, g : g + 1, :] = value
            own = (
                jnp.sum(query.astype(jnp.float32) * key, axis=1, keepdims=True) * inverse_root
            )
            raw = dot_nt(query, kbuf[s, g])
            key_row = scale_row(kscale, s, g, cache_len // blocks, blocks)
            value_row = scale_row(vscale, s, g, cache_len // blocks, blocks)
            scores = jnp.where(live, raw * key_row * inverse_root, -jnp.inf)
            top = jnp.maximum(jnp.max(scores, axis=1, keepdims=True), own)
            exps = jnp.exp(scores - top)
            own_exp = jnp.exp(own - top)
            denominator = jnp.sum(exps, axis=1, keepdims=True) + own_exp
            weights = (exps * value_row / denominator).astype(jnp.bfloat16)
            own_weight = (own_exp / denominator).astype(jnp.bfloat16).astype(jnp.float32)
            mixed = jnp.dot(weights, vbuf[s, g], preferred_element_type=jnp.float32)
            mixed = mixed + own_weight * value
            for j in range(group // share):
                asnd[(g * group) // share + j, s] = mixed[j * share : (j + 1) * share].astype(
                    jnp.bfloat16
                )


def layer_kernel(
    nt, hid, gain, slots, qgain, kgain, lens, kscale, vscale, cosine, sine, mgain,
    wq, kc, vc, wo, wg, wu, wd, out, kvout,
    wqb, kb, vb, wob, wgb, wub, wdb, gath, part, half, send2, recv2, total, acc, snd, rcv,
    grid, newkv, asnd, arcv, heads, gacc, uacc, wsem, bsem, asem, gsem, psem, ssem,
):
    mt = lax.axis_index("tensor")
    mh = lax.axis_index("head")
    chunks, tile = part.shape[0], part.shape[3]
    keep = wdb.shape[0]
    spare = wd.shape[0] - keep
    requests = acc.shape[0]

    def rows_of(c):
        span = pl.ds(pl.multiple_of(c * tile, tile), tile)
        return pltpu.make_async_copy(wq.at[0, span, :], wqb.at[span, :], wsem.at[0, c])

    def columns_of(src, dst, i, c):
        span = pl.ds(pl.multiple_of(c * tile, tile), tile)
        return pltpu.make_async_copy(src.at[:, span], dst.at[:, span], wsem.at[i, c])

    down = wd.at[pl.ds(0, keep), :]
    tail = pltpu.make_async_copy(
        wd.at[pl.ds(keep, spare), :], wob.at[pl.ds(0, spare), :], bsem.at[2]
    )
    key_copy = pltpu.make_async_copy(kc, kb, bsem.at[0])
    value_copy = pltpu.make_async_copy(vc, vb, bsem.at[1])
    for c in range(chunks):
        rows_of(c).start()
    key_copy.start()
    value_copy.start()
    for c in range(chunks):
        columns_of(wo.at[0], wob, 1, c).start()
    greet(mt, mh, nt)
    own = rms_scale(hid[...].astype(jnp.float32), gain[...]).astype(jnp.bfloat16)
    gather_rows(own, gath, part, [gsem.at[0, i] for i in range(4)], mt, mh, nt)
    for c in range(chunks):
        columns_of(wg, wgb, 2, c).start()
        columns_of(wu, wub, 3, c).start()
    acc[...] = jnp.zeros_like(acc)

    def gathered(c):
        return part[c].reshape(requests, tile).astype(jnp.bfloat16)

    @pl.loop(0, chunks)
    def _(c):
        span = pl.ds(pl.multiple_of(c * tile, tile), tile)
        rows_of(c).wait()
        acc[...] += jnp.dot(gathered(c), wqb[span, :], preferred_element_type=jnp.float32)

    shape = (requests, requests)
    down_iota = lax.broadcasted_iota(jnp.int32, shape, 0)
    across = lax.broadcasted_iota(jnp.int32, shape, 1)
    rows = hid.shape[0]
    half_lines = requests // 2
    request_at = (
        lax.div(lax.rem(across, half_lines), rows) * (2 * rows)
        + lax.div(across, half_lines) * rows
        + lax.rem(across, rows)
    )
    place = jnp.where(down_iota == request_at, 1.0, 0.0).astype(jnp.bfloat16)
    by_slot = jnp.where(down_iota == slots[...], 1.0, 0.0).astype(jnp.bfloat16)
    pick = jnp.dot(by_slot, place, preferred_element_type=jnp.float32).astype(jnp.bfloat16)
    acc[...] = jnp.dot(pick, acc[...].astype(jnp.bfloat16), preferred_element_type=jnp.float32)
    per = requests // nt
    for t in range(nt):
        snd[t] = acc[t * per : (t + 1) * per, :].astype(jnp.bfloat16)
    exchange(snd, rcv, asem.at[0], mt, mh, nt)
    for c in range(chunks):
        columns_of(down, wdb, 4, c).start()
    key_copy.wait()
    value_copy.wait()
    attend(
        rcv, grid, newkv, asnd, kb, vb, lens, kscale, vscale, qgain, kgain, cosine, sine
    )
    exchange(asnd, arcv, asem.at[1], mt, mh, nt)
    kvout[...] = newkv[...].astype(jnp.bfloat16)
    share, head_dim = asnd.shape[2], asnd.shape[3]
    for t in range(nt):
        for s in range(per):
            values = arcv[t, s].astype(jnp.float32)
            for j in range(share):
                heads[t * per + s : t * per + s + 1, j * head_dim : (j + 1) * head_dim] = values[
                    j : j + 1, :
                ]
    attended = lax.dot_general(
        pick,
        heads[...].astype(jnp.bfloat16),
        (((0,), (0,)), ((), ())),
        preferred_element_type=jnp.float32,
    ).astype(jnp.bfloat16)

    def project(c):
        span = pl.ds(pl.multiple_of(c * tile, tile), tile)
        columns_of(wo.at[0], wob, 1, c).wait()
        return jnp.dot(attended, wob[:, span], preferred_element_type=jnp.float32)

    matmul_scatter(
        project, part, half, send2, recv2, total,
        [psem.at[0, 0], psem.at[0, 1], ssem.at[0, 0], ssem.at[0, 1]], mt, mh, nt,
    )
    tail.start()
    middle = (total[...] + hid[...].astype(jnp.float32)).astype(jnp.bfloat16).astype(jnp.float32)
    normed = rms_scale(middle, mgain[...]).astype(jnp.bfloat16)
    gather_rows(normed, gath, part, [gsem.at[1, i] for i in range(4)], mt, mh, nt)
    gacc[...] = jnp.zeros_like(gacc)
    uacc[...] = jnp.zeros_like(uacc)

    @pl.loop(0, chunks)
    def _(c):
        span = pl.ds(pl.multiple_of(c * tile, tile), tile)
        lhs = gathered(c)
        columns_of(wg, wgb, 2, c).wait()
        gacc[...] += dot_nt(lhs, wgb[:, span])
        columns_of(wu, wub, 3, c).wait()
        uacc[...] += dot_nt(lhs, wub[:, span])

    gate = gacc[...]
    gacc[...] = gate / (1.0 + jnp.exp(-gate)) * uacc[...]
    active = gacc[...].astype(jnp.bfloat16)
    tail.wait()

    def lower(c):
        span = pl.ds(pl.multiple_of(c * tile, tile), tile)
        columns_of(down, wdb, 4, c).wait()
        return jnp.dot(
            active[:, :keep], wdb[:, span], preferred_element_type=jnp.float32
        ) + jnp.dot(active[:, keep:], wob[:spare, span], preferred_element_type=jnp.float32)

    matmul_scatter(
        lower, part, half, send2, recv2, total,
        [psem.at[1, 0], psem.at[1, 1], ssem.at[1, 0], ssem.at[1, 1]], mt, mh, nt,
    )
    out[...] = (middle + total[...]).astype(jnp.bfloat16)


def kept_rows(w_out, w_down):
    return -(-(w_down.shape[0] - w_out.shape[1]) // 128) * 128


def fused_layer(
    nt, hidden_state, input_gain, w_qkv, query_gain, key_gain, slot_of, lengths, key_cache,
    value_cache, key_scale, value_scale, w_out, middle_gain, w_gate, w_up, w_down,
):
    rows, width = hidden_state.shape
    requests = rows * nt * 2
    cols = w_qkv.shape[2]
    per = requests // nt
    chunks = 5
    tile = width // chunks
    units = w_gate.shape[1]
    kv_local, head_dim = key_cache.shape[1], key_cache.shape[3]
    group = cols * nt // (kv_local * head_dim) - 2
    share = kv_local * group // nt
    keep = kept_rows(w_out, w_down)
    frequency = jnp.power(
        jnp.float32(THETA), -jnp.arange(head_dim // 2, dtype=jnp.float32) * 2.0 / head_dim
    )
    angles = lengths.astype(jnp.float32)[:, None] * frequency
    cosine, sine = jnp.cos(angles), jnp.sin(angles)
    cosine = jnp.concatenate([cosine, cosine], axis=1)
    sine = jnp.concatenate([-sine, sine], axis=1)
    vmem = pl.BlockSpec(memory_space=pltpu.VMEM)
    smem = pl.BlockSpec(memory_space=pltpu.SMEM)
    anyspace = pl.BlockSpec(memory_space=pl.ANY)
    dma = pltpu.SemaphoreType.DMA
    bf16, f32 = jnp.bfloat16, jnp.float32
    line = lambda a: a.reshape(1, -1)
    return pl.pallas_call(
        functools.partial(layer_kernel, nt),
        out_shape=(
            jax.ShapeDtypeStruct((rows, width), bf16),
            jax.ShapeDtypeStruct((per, 2, kv_local, head_dim), bf16),
        ),
        in_specs=[vmem] * 5 + [smem] * 3 + [vmem] * 3 + [anyspace] * 7,
        out_specs=(vmem, vmem),
        scratch_shapes=[
            pltpu.VMEM((width, cols), bf16),
            pltpu.VMEM(key_cache.shape, bf16),
            pltpu.VMEM(value_cache.shape, bf16),
            pltpu.VMEM((w_out.shape[1], width), bf16),
            pltpu.VMEM((units, width), bf16),
            pltpu.VMEM((units, width), bf16),
            pltpu.VMEM((keep, width), bf16),
            pltpu.VMEM((2, nt, rows, width), bf16),
            pltpu.VMEM((chunks, 2, requests // 2, tile), f32),
            pltpu.VMEM((chunks, requests // 2, tile), f32),
            pltpu.VMEM((chunks, nt, rows, tile), bf16),
            pltpu.VMEM((chunks, nt, rows, tile), bf16),
            pltpu.VMEM((rows, width), f32),
            pltpu.VMEM((requests, cols), f32),
            pltpu.VMEM((nt, per, cols), bf16),
            pltpu.VMEM((nt, per, cols), bf16),
            pltpu.VMEM((per * kv_local, 16, head_dim), f32),
            pltpu.VMEM((per, 2, kv_local, head_dim), f32),
            pltpu.VMEM((nt, per, share, head_dim), bf16),
            pltpu.VMEM((nt, per, share, head_dim), bf16),
            pltpu.VMEM((requests, w_out.shape[1]), f32),
            pltpu.VMEM((requests, units), f32),
            pltpu.VMEM((requests, units), f32),
            dma((5, chunks)),
            dma((3,)),
            dma((2, 2, nt)),
            dma((2, 4, nt)),
            dma((2, 2, chunks)),
            dma((2, 2, chunks, nt)),
        ],
        compiler_params=pltpu.CompilerParams(
            collective_id=0, has_side_effects=True, vmem_limit_bytes=VMEM_LIMIT
        ),
    )(
        hidden_state, line(input_gain), line(slot_of), line(query_gain), line(key_gain),
        lengths, key_scale.transpose(2, 0, 1), value_scale.transpose(2, 0, 1), cosine, sine,
        line(middle_gain),
        w_qkv, key_cache, value_cache, w_out, w_gate.T, w_up.T, w_down,
    )


def kernels_fit(nt, nh, hidden_state, w_qkv, key_cache, w_out, w_gate, w_down):
    width = hidden_state.shape[1]
    kv_local, head_dim = key_cache.shape[1], key_cache.shape[3]
    cols = w_qkv.shape[2]
    if nh != 2 or head_dim != 128 or cols % head_dim or w_out.shape[1] % head_dim:
        return False
    if width % 640 or w_gate.shape[1] % 16 or cols * nt % (kv_local * head_dim):
        return False
    group = cols * nt // (kv_local * head_dim) - 2
    share = kv_local * group // nt
    if group != 8 or share == 0 or group % share:
        return False
    keep = kept_rows(w_out, w_down)
    if not 0 < keep < w_down.shape[0]:
        return False
    weights = width * (cols + w_out.shape[1] + 2 * w_gate.shape[1] + keep)
    caches = 2 * math.prod(key_cache.shape)
    others = 2 * nt * hidden_state.shape[0] * width * 14
    return 2 * (weights + caches) + others < VMEM_LIMIT


def per_device(
    nt,
    nh,
    hidden_state,
    input_gain,
    w_qkv,
    query_gain,
    key_gain,
    slot_of,
    lengths,
    key_cache,
    value_cache,
    key_scale,
    value_scale,
    w_out,
    middle_gain,
    w_gate,
    w_up,
    w_down,
):
    rows_local = hidden_state.shape[0]
    requests = slot_of.shape[0]
    if kernels_fit(nt, nh, hidden_state, w_qkv, key_cache, w_out, w_gate, w_down):
        return fused_layer(
            nt, hidden_state, input_gain, w_qkv, query_gain, key_gain, slot_of, lengths,
            key_cache, value_cache, key_scale, value_scale, w_out, middle_gain, w_gate, w_up,
            w_down,
        )
    normed_in = rms_scale(hidden_state.astype(jnp.float32), input_gain).astype(jnp.bfloat16)
    qkv_weights = w_qkv[0]
    qkv_local = jnp.dot(
        lax.all_gather(normed_in, ("tensor", "head"), axis=0, tiled=True),
        qkv_weights,
        preferred_element_type=jnp.float32,
    ).astype(jnp.bfloat16)
    request_of = (
        jnp.zeros((requests,), jnp.int32).at[slot_of].set(jnp.arange(requests, dtype=jnp.int32))
    )
    qkv_slots = jnp.take(qkv_local, request_of, axis=0)
    owned_rows = lax.all_to_all(qkv_slots, "tensor", split_axis=0, concat_axis=1, tiled=True)
    slots_here = owned_rows.shape[0]
    kv_local = key_cache.shape[1]
    cache_len = key_cache.shape[2]
    head_dim = key_cache.shape[3]
    block_size = cache_len // key_scale.shape[2]
    group_size = owned_rows.shape[1] // (kv_local * head_dim) - 2
    grouped = owned_rows.reshape(slots_here, kv_local, group_size + 2, head_dim)
    queries = grouped[:, :, :group_size].astype(jnp.float32)
    keys_new = grouped[:, :, group_size].astype(jnp.float32)
    values_new = grouped[:, :, group_size + 1]
    query_rot = rotate(rms_scale(queries, query_gain), lengths[:, None, None]).astype(jnp.bfloat16)
    key_rot = rotate(rms_scale(keys_new, key_gain), lengths[:, None]).astype(jnp.bfloat16)
    new_kv = jnp.stack([key_rot, values_new], axis=1)
    inverse_root = 1.0 / math.sqrt(head_dim)
    own_scores = (
        jnp.einsum("rgih,rgh->rgi", query_rot, key_rot, preferred_element_type=jnp.float32)
        * inverse_root
    )
    value_expand = jnp.repeat(value_scale, block_size, axis=2)
    key_expand = jnp.repeat(key_scale, block_size, axis=2)
    positions = jnp.arange(cache_len, dtype=jnp.int32)
    live_mask = positions[None, None, None, :] < lengths[:, None, None, None]
    raw_scores = jnp.einsum(
        "rgih,rgph->rgip", query_rot, key_cache, preferred_element_type=jnp.float32
    )
    cache_scores = jnp.where(
        live_mask, raw_scores * key_expand[:, :, None, :] * inverse_root, -jnp.inf
    )
    cache_weights, own_weights = softmax_weights(cache_scores, own_scores, value_expand)
    mixed_sum = jnp.einsum(
        "rgip,rgph->rgih", cache_weights, value_cache, preferred_element_type=jnp.float32
    )
    mixed_sum = (
        mixed_sum
        + own_weights.astype(jnp.float32)[..., None] * values_new.astype(jnp.float32)[:, :, None, :]
    )
    attended = mixed_sum.astype(jnp.bfloat16).reshape(slots_here, kv_local * group_size * head_dim)
    returned = lax.all_to_all(attended, "tensor", split_axis=1, concat_axis=0, tiled=True)
    by_request = jnp.take(returned, slot_of, axis=0)
    out_weights = w_out[0]
    own_offset = lax.axis_index(("tensor", "head")) * rows_local
    partial_out = jnp.dot(by_request, out_weights, preferred_element_type=jnp.float32)
    own_rows = lax.dynamic_slice_in_dim(
        partial_out, own_offset, rows_local, 0
    ) + hidden_state.astype(jnp.float32)
    with_residual = lax.dynamic_update_slice_in_dim(partial_out, own_rows, own_offset, 0)
    summed = lax.psum(with_residual, ("tensor", "head"))
    middle_all = summed.astype(jnp.bfloat16)
    normed_mid = rms_scale(middle_all.astype(jnp.float32), middle_gain).astype(jnp.bfloat16)
    activation = gate_units(normed_mid, w_gate, w_up)
    middle = lax.dynamic_slice_in_dim(middle_all, own_offset, rows_local, 0)
    reduced = lax.psum_scatter(
        jnp.dot(activation, w_down, preferred_element_type=jnp.float32),
        ("tensor", "head"),
        scatter_dimension=0,
        tiled=True,
    )
    layer_out = (middle.astype(jnp.float32) + reduced).astype(jnp.bfloat16)
    return (layer_out, new_kv)


def solution(mesh):
    return jax.shard_map(
        functools.partial(per_device, mesh.shape["tensor"], mesh.shape["head"]),
        mesh=mesh,
        in_specs=(
            P(("groups", "tensor", "head"), None),
            P(),
            P("head", None, "tensor"),
            P(),
            P(),
            P("groups"),
            P(("groups", "tensor")),
            P(("groups", "tensor"), "head", None, None),
            P(("groups", "tensor"), "head", None, None),
            P(("groups", "tensor"), "head", None),
            P(("groups", "tensor"), "head", None),
            P("head", "tensor", None),
            P(),
            P(None, ("tensor", "head")),
            P(None, ("tensor", "head")),
            P(("tensor", "head"), None),
        ),
        out_specs=(
            P(("groups", "tensor", "head"), None),
            P(("groups", "tensor"), None, "head", None),
        ),
        check_vma=False,
    )
```
